128 devices in a mesh: row: 2 (over core), col: 64 (over z, y, x).
Axes of the slice: x: 4, y: 4, z: 4, core: 2. Of those that a mesh axis runs over, the one named last changes fastest.
Arguments:
- features: bfloat16 [512, 8192], P('col', 'row'), may hold values from -6 to 6
- a_blocks: bfloat16 [64, 2, 2, 128, 128], P('row'), may hold values from -0.375 to 0.375
- block_cols: int32 [64, 2, 2], P('row'), may hold values from 0 to 31
- block_counts: int32 [64, 2], P('row'), may hold values from 0 to 2
- weight: bfloat16 [512, 512], P('col'), may hold values from -0.25 to 0.25
- cotangent: bfloat16 [512, 8192], P('col', 'row'), may hold values from -6 to 6
Outputs:
- output: bfloat16 [512, 8192], P('col', 'row')
- grad_weight: float32 [512, 512], P('col')
- grad_features: bfloat16 [512, 8192], P('col', 'row')
The draws below stay inside these ranges and needn't reach their ends.
Inputs may be any that keep to these rules, and one draw needn't show every extreme that they name: `block_cols`: block column indices lie within one slab's blocks.
All inputs are finite; a program needn't handle non-finite values.
Results may differ from the reference program's by a relative error of at most 0.0061.
Values may be sent and summed in bfloat16 or wider, within the bound.
No kernel may reach another device: no remote copies, remote signals or barrier semaphores. Data moves between devices by JAX's collectives and lax.ppermute only.
A program may use at most 128 MiB of HBM per device.

```python
import jax
import jax.numpy as jnp
from jax import lax

F = 512
BLOCK = 128
KB = 2
ROWS_DEV = 4096
SECTIONS = 2
NODES = 8192
NBLOCKS = 64


def with_ends(values, key, least, high):
    extent = values.shape
    spot = [jax.random.randint(jax.random.fold_in(key, axis), (), 0, extent[axis]) for axis in range(len(extent))]
    values = values.at[tuple(spot)].set(least)
    longest = extent.index(max(extent))
    spot[longest] = (spot[longest] + 1) % extent[longest]
    return values.at[tuple(spot)].set(high)


def steps_of(stream_key, extent, shards, low, top_value):
    def one(axis_at, blocks):
        steps = jax.random.uniform(jax.random.fold_in(jax.random.fold_in(stream_key, 6), axis_at), (blocks,), jnp.float32, low / len(shards), top_value / len(shards))
        return jnp.repeat(jnp.exp(steps), extent[axis_at] // blocks).reshape((-1,) + (1,) * (len(extent) - axis_at - 1))

    level = one(*shards[0])
    for cut in shards[1:]:
        level = level * one(*cut)
    return level


def gaussian(stream_key, extent, width, limit, pieces=(), held_as=jnp.bfloat16):
    loudness = steps_of(stream_key, extent, pieces, -0.22, 0.18) if pieces else 1.0
    result = jax.random.normal(stream_key, extent, jnp.float32) * width * loudness
    return jnp.minimum(jnp.maximum(result, -limit), limit).astype(held_as)


def setup_inputs(seed: int = 0) -> dict:
    key_of = jax.random.split(jax.random.key(seed), 7)
    features = gaussian(key_of[0], (F, NODES), 1.0, 6.0, ((0, 64), (1, 2)))
    a_blocks = gaussian(key_of[1], (NBLOCKS, SECTIONS, KB, BLOCK, BLOCK), (SECTIONS * KB * BLOCK // 2) ** -0.5, 0.375, ((0, 2),))
    block_cols = with_ends(jax.random.randint(key_of[2], (NBLOCKS, SECTIONS, KB), 0, ROWS_DEV // BLOCK), jax.random.fold_in(key_of[2], 1), 0, (ROWS_DEV // BLOCK) - 1).astype(jnp.int32)
    block_counts = with_ends(jax.random.randint(key_of[3], (NBLOCKS, SECTIONS), 0, KB + 1), jax.random.fold_in(key_of[3], 1), 0, KB).astype(jnp.int32)
    weight = gaussian(key_of[4], (F, F), F ** -0.5, 0.25, ((0, 64),))
    cotangent = gaussian(key_of[5], (F, NODES), 1.0, 6.0, ((0, 64), (1, 2)))
    return {"features": features, "a_blocks": a_blocks, "block_cols": block_cols, "block_counts": block_counts, "weight": weight, "cotangent": cotangent}


def reference(features, a_blocks, block_cols, block_counts, weight, cotangent):
    row_blocks = ROWS_DEV // BLOCK
    all_blocks = NODES // BLOCK
    global_index = (jnp.arange(SECTIONS, dtype=jnp.int32)[None, :, None] * row_blocks + block_cols).astype(jnp.int32)
    slot_ids = jnp.arange(KB, dtype=jnp.int32)
    panels = features.reshape(F, all_blocks, BLOCK).astype(jnp.float32)

    def masked_of(blocks, counts):
        live_mask = (slot_ids[None, :] < counts[:, None]).astype(jnp.float32)
        return blocks.astype(jnp.float32) * live_mask[:, :, None, None]

    def forward_one(packed):
        blocks, index_one, counts = packed
        picked = panels[:, index_one]
        return jnp.einsum('fskj,skij->fi', picked, masked_of(blocks, counts))
    gathered = lax.map(forward_one, (a_blocks, global_index, block_counts))
    aggregated = jnp.transpose(gathered, (1, 0, 2)).reshape(F, NODES).astype(jnp.bfloat16)
    preact = jnp.dot(weight, aggregated, preferred_element_type=jnp.float32)
    output = jax.nn.silu(preact).astype(jnp.bfloat16)
    sigmoid_pre = jax.nn.sigmoid(preact)
    dpre = (cotangent.astype(jnp.float32) * sigmoid_pre * (1.0 + preact * (1.0 - sigmoid_pre))).astype(jnp.bfloat16)
    grad_weight = lax.dot_general(dpre, aggregated, (((1,), (1,)), ((), ())), preferred_element_type=jnp.float32)
    grad_weight = grad_weight / jnp.sqrt(jnp.float32(NODES))
    dagg = lax.dot_general(weight, dpre, (((0,), (0,)), ((), ())), preferred_element_type=jnp.float32).astype(jnp.bfloat16)
    dagg_blocks = jnp.transpose(dagg.reshape(F, all_blocks, BLOCK), (1, 0, 2)).astype(jnp.float32)

    def back_one(total, packed):
        blocks, index_one, counts, grad_rows = packed
        contrib = jnp.einsum('fi,skij->fskj', grad_rows, masked_of(blocks, counts))
        return (total.at[:, index_one].add(contrib), None)
    start_total = jnp.zeros((F, all_blocks, BLOCK), jnp.float32)
    total, unused = lax.scan(back_one, start_total, (a_blocks, global_index, block_counts, dagg_blocks))
    grad_features = total.reshape(F, NODES).astype(jnp.bfloat16)
    return (output, grad_weight, grad_features)
```

```python
import functools

import jax
import jax.numpy as jnp
from jax import lax
from jax.experimental import pallas as pl
from jax.experimental.pallas import tpu as pltpu
from jax.sharding import PartitionSpec as P

STEPS = 4
SWAP = [(0, 1), (1, 0)]


def lower_half(shape):
    return lax.broadcasted_iota(jnp.int32, shape, len(shape) - 1) < shape[-1] // 2


def halves(a, b):
    mask = lower_half(a.shape)
    half = a.shape[-1] // 2
    return (
        jnp.where(mask, a, pltpu.roll(b, half, a.ndim - 1)),
        jnp.where(mask, pltpu.roll(a, half, a.ndim - 1), b),
    )


def gather_kernel(cols, counts, own, other, a_ref, weight, cot, msg, feats):
    step = pl.program_id(0)
    per = a_ref.shape[0]
    row = lax.axis_index("row")

    @pl.when(step == 0)
    def _():
        feats[row] = own[...]
        feats[1 - row] = other[...]

    for i in range(per):
        b = step * per + i
        total = jnp.zeros((8, 128), jnp.float32)
        for s in range(2):
            for k in range(2):
                col = pl.multiple_of(cols[b, s * 2 + k] * 128, 128)
                x = feats[s, :, pl.ds(col, 128)]
                x = lax.select(k < counts[b, s], x, jnp.zeros_like(x))
                total += lax.dot_general(
                    x, a_ref[i, s, k], (((1,), (1,)), ((), ())), preferred_element_type=jnp.float32
                )
        first, second = halves(total, cot[:, i * 128 : (i + 1) * 128].astype(jnp.float32))
        msg[2 * i, :, :128] = first.astype(jnp.bfloat16)
        msg[2 * i + 1, :, :128] = second.astype(jnp.bfloat16)
    w = weight[...]
    for i in range(2 * per):
        msg[i, :, 128:] = w


def dense_kernel(msg, back):
    w = msg[:, 128:]
    pair = msg[:, :128]
    pre = jnp.dot(w, pair, preferred_element_type=jnp.float32)
    cot = pltpu.roll(pair.astype(jnp.float32), 64, 1)
    sig = jax.nn.sigmoid(pre)
    out = pre * sig
    dpre = cot * sig * (1.0 + pre * (1.0 - sig))
    dpre = jnp.where(lower_half(dpre.shape), dpre, 0.0).astype(jnp.bfloat16)
    dagg = lax.dot_general(w, dpre, (((0,), (0,)), ((), ())), preferred_element_type=jnp.float32)
    back[:, :128] = jnp.where(lower_half(out.shape), out, pltpu.roll(dagg, 64, 1)).astype(jnp.bfloat16)
    grad = lax.dot_general(dpre, pair, (((1,), (1,)), ((), ())), preferred_element_type=jnp.float32)
    back[:, 128:] = grad.astype(jnp.bfloat16)


def scatter_kernel(cols, counts, back, a_ref, out, own, send, terms, grad):
    step = pl.program_id(0)
    per = a_ref.shape[0]
    row = lax.axis_index("row")

    @pl.when(step == 0)
    def _():
        terms[...] = jnp.zeros_like(terms)
        grad[...] = jnp.zeros_like(grad)

    part = jnp.zeros(grad.shape, jnp.float32)
    for i in range(2 * per):
        part += back[i, :, 128:].astype(jnp.float32)
    grad[...] += part
    for i in range(per):
        b = step * per + i
        outs, dagg = halves(
            back[2 * i, :, :128].astype(jnp.float32), back[2 * i + 1, :, :128].astype(jnp.float32)
        )
        out[:, i * 128 : (i + 1) * 128] = outs.astype(jnp.bfloat16)
        dagg = dagg.astype(jnp.bfloat16)
        for s in range(2):
            for k in range(2):
                col = pl.multiple_of(cols[b, s * 2 + k] * 128, 128)
                term = jnp.dot(dagg, a_ref[i, s, k], preferred_element_type=jnp.float32)
                term = lax.select(k < counts[b, s], term, jnp.zeros_like(term))
                terms[s, :, pl.ds(col, 128)] += term

    @pl.when(step == pl.num_programs(0) - 1)
    def _():
        own[:, :4096] = terms[row]
        own[:, 4096:] = grad[...]
        send[:, :4096] = terms[1 - row]
        send[:, 4096:] = grad[...]


def merge_kernel(scale, own, other, grad_features, grad_weight):
    total = own[...] + other[...]
    grad_features[...] = total[:, :4096].astype(jnp.bfloat16)
    grad_weight[...] = total[:, 4096:] * scale


def local(features, a_blocks, block_cols, block_counts, weight, cotangent):
    fd, slab = features.shape
    nb = a_blocks.shape[0]
    width = weight.shape[1]
    col = lax.axis_size("col")
    per = nb // STEPS
    smem = pl.BlockSpec(memory_space=pltpu.SMEM)
    cols = block_cols.reshape(nb, 4)
    a_spec = pl.BlockSpec((per, 2, 2, 128, 128), lambda t: (t, 0, 0, 0, 0))
    whole = lambda *shape: pl.BlockSpec(shape, lambda t: (0,) * len(shape))
    msg_spec = pl.BlockSpec((2 * per, fd, 128 + width), lambda t: (t, 0, 0))
    lanes = pl.BlockSpec((fd, per * 128), lambda t: (0, t))

    other = lax.ppermute(features, "row", SWAP)
    msg = pl.pallas_call(
        gather_kernel,
        grid=(STEPS,),
        in_specs=[smem, smem, whole(fd, slab), whole(fd, slab), a_spec, whole(fd, width), lanes],
        out_specs=msg_spec,
        out_shape=jax.ShapeDtypeStruct((col, fd, 128 + width), jnp.bfloat16),
        scratch_shapes=[pltpu.VMEM((2, fd, slab), jnp.bfloat16)],
        name="gather",
    )(cols, block_counts, features, other, a_blocks, weight, cotangent)
    msg = lax.all_to_all(msg.reshape(col * fd, 128 + width), "col", 0, 0, tiled=True)
    back = pl.pallas_call(
        dense_kernel,
        out_shape=jax.ShapeDtypeStruct(msg.shape, jnp.bfloat16),
        name="dense",
    )(msg)
    back = lax.all_to_all(back, "col", 0, 0, tiled=True).reshape(col, fd, 128 + width)
    part = jax.ShapeDtypeStruct((fd, slab + width), jnp.float32)
    output, own, send = pl.pallas_call(
        scatter_kernel,
        grid=(STEPS,),
        in_specs=[smem, smem, msg_spec, a_spec],
        out_specs=[lanes, whole(fd, slab + width), whole(fd, slab + width)],
        out_shape=[jax.ShapeDtypeStruct((fd, slab), jnp.bfloat16), part, part],
        scratch_shapes=[pltpu.VMEM((2, fd, slab), jnp.float32), pltpu.VMEM((fd, width), jnp.float32)],
        name="scatter",
    )(cols, block_counts, back, a_blocks)
    got = lax.ppermute(send, "row", SWAP)
    scale = 1.0 / (slab * lax.axis_size("row")) ** 0.5
    grad_features, grad_weight = pl.pallas_call(
        functools.partial(merge_kernel, scale),
        out_shape=[
            jax.ShapeDtypeStruct((fd, slab), jnp.bfloat16),
            jax.ShapeDtypeStruct((fd, width), jnp.float32),
        ],
        name="merge",
    )(own, got)
    return output, grad_weight, grad_features


def solution(mesh):
    placed = (
        P("col", "row"),
        P("row", None, None, None, None),
        P("row", None, None),
        P("row", None),
        P("col", None),
        P("col", "row"),
    )
    return jax.shard_map(
        local,
        mesh=mesh,
        in_specs=placed,
        out_specs=(P("col", "row"), P("col", None), P("col", "row")),
        check_vma=False,
    )
```

```python
import functools

import jax
import jax.numpy as jnp
from jax import lax
from jax.experimental import pallas as pl
from jax.experimental.pallas import tpu as pltpu
from jax.sharding import PartitionSpec as P

SWAP = [(0, 1), (1, 0)]
VMEM_LIMIT = 4 << 20
CHUNKS = 4


def lower_half(shape):
    return lax.broadcasted_iota(jnp.int32, shape, len(shape) - 1) < shape[-1] // 2


def halves(a, b):
    mask = lower_half(a.shape)
    half = a.shape[-1] // 2
    return (
        jnp.where(mask, a, pltpu.roll(b, half, a.ndim - 1)),
        jnp.where(mask, pltpu.roll(a, half, a.ndim - 1), b),
    )


def first_kernel(cols_hbm, counts_hbm, own_hbm, a_hbm, a_ref, total, own, cols, counts, sems):
    row = lax.axis_index("row")
    blocks = a_ref.shape[0]
    per = blocks // CHUNKS
    small = [
        pltpu.make_async_copy(src, dst, sems.at[i])
        for i, (src, dst) in enumerate(((cols_hbm, cols), (counts_hbm, counts), (own_hbm, own)))
    ]
    large = [
        pltpu.make_async_copy(
            a_hbm.at[pl.ds(c * per, per)], a_ref.at[pl.ds(c * per, per)], sems.at[len(small) + c]
        )
        for c in range(CHUNKS)
    ]
    for copy in small + large:
        copy.start()
    for copy in small:
        copy.wait()
    for b in range(blocks):
        if b % per == 0:
            large[b // per].wait()
        total[:, b * 128 : (b + 1) * 128] = aggregate(cols, counts, own, a_ref, row, b)


def aggregate(cols, counts, feats, a_ref, s, b):
    total = jnp.zeros((8, 128), jnp.float32)
    for k in range(2):
        col = pl.multiple_of(cols[s, k, b] * 128, 128)
        x = feats[:, pl.ds(col, 128)]
        x = lax.select(k < counts[s, b], x, jnp.zeros_like(x))
        total += lax.dot_general(
            x, a_ref[b, s, k], (((1,), (1,)), ((), ())), preferred_element_type=jnp.float32
        )
    return total


def second_kernel(cols, counts, other, a_ref, part, weight, cot, msg):
    row = lax.axis_index("row")
    for b in range(a_ref.shape[0]):
        here = slice(b * 128, (b + 1) * 128)
        total = part[:, here] + aggregate(cols, counts, other, a_ref, 1 - row, b)
        total = total.astype(jnp.bfloat16).astype(jnp.float32)
        first, second = halves(total, cot[:, here].astype(jnp.float32))
        msg[2 * b, :, :128] = first.astype(jnp.bfloat16)
        msg[2 * b + 1, :, :128] = second.astype(jnp.bfloat16)
    w = weight[...]
    for b in range(msg.shape[0]):
        msg[b, :, 128:] = w


def dense_kernel(msg, back):
    w = msg[:, 128:]
    pair = msg[:, :128]
    pre = jnp.dot(w, pair, preferred_element_type=jnp.float32)
    cot = pltpu.roll(pair.astype(jnp.float32), 64, 1)
    sig = jax.nn.sigmoid(pre)
    out = pre * sig
    dpre = cot * sig * (1.0 + pre * (1.0 - sig))
    dpre = jnp.where(lower_half(dpre.shape), dpre, 0.0).astype(jnp.bfloat16)
    dagg = lax.dot_general(w, dpre, (((0,), (0,)), ((), ())), preferred_element_type=jnp.float32)
    back[:, :128] = jnp.where(lower_half(out.shape), out, pltpu.roll(dagg, 64, 1)).astype(jnp.bfloat16)
    grad = lax.dot_general(dpre, pair, (((1,), (1,)), ((), ())), preferred_element_type=jnp.float32)
    back[:, 128:] = grad.astype(jnp.bfloat16)


def spread(cols, counts, dagg, a_ref, s, b, terms):
    for k in range(2):
        col = pl.multiple_of(cols[s, k, b] * 128, 128)
        term = jnp.dot(dagg, a_ref[b, s, k], preferred_element_type=jnp.float32)
        term = lax.select(k < counts[s, b], term, jnp.zeros_like(term))
        terms[:, pl.ds(col, 128)] += term


def send_kernel(cols, counts, back, a_ref, send, dagg_ref):
    row = lax.axis_index("row")
    blocks = a_ref.shape[0]
    slab = blocks * 128
    send[...] = jnp.zeros_like(send)
    for b in range(blocks):
        _, dagg = halves(
            back[2 * b, :, :128].astype(jnp.float32), back[2 * b + 1, :, :128].astype(jnp.float32)
        )
        dagg = dagg.astype(jnp.bfloat16)
        dagg_ref[:, b * 128 : (b + 1) * 128] = dagg
        spread(cols, counts, dagg, a_ref, 1 - row, b, send)
    grad = jnp.zeros((send.shape[0], send.shape[1] - slab), jnp.float32)
    for b in range(2 * blocks):
        grad += back[b, :, 128:].astype(jnp.float32)
    send[:, slab:] = grad


def keep_kernel(cols, counts, back, a_ref, dagg_ref, out, own):
    row = lax.axis_index("row")
    own[...] = jnp.zeros_like(own)
    for b in range(a_ref.shape[0]):
        here = slice(b * 128, (b + 1) * 128)
        outs, _ = halves(
            back[2 * b, :, :128].astype(jnp.float32), back[2 * b + 1, :, :128].astype(jnp.float32)
        )
        out[:, here] = outs.astype(jnp.bfloat16)
        spread(cols, counts, dagg_ref[:, here], a_ref, row, b, own)


def merge_kernel(scale, own, sent, got, grad_features, grad_weight):
    slab = own.shape[1]
    grad_features[...] = (own[...] + got[:, :slab]).astype(jnp.bfloat16)
    grad_weight[...] = (sent[:, slab:] + got[:, slab:]) * scale


def call(kernel, name, scalars, arrays, outs):
    vmem = pl.BlockSpec(memory_space=pltpu.VMEM)
    smem = pl.BlockSpec(memory_space=pltpu.SMEM)
    return pl.pallas_call(
        kernel,
        in_specs=[smem] * len(scalars) + [vmem] * len(arrays),
        out_specs=[vmem] * len(outs),
        out_shape=[jax.ShapeDtypeStruct(shape, dtype) for shape, dtype in outs],
        compiler_params=pltpu.CompilerParams(vmem_limit_bytes=VMEM_LIMIT),
        name=name,
    )(*scalars, *arrays)


def local(features, a_blocks, block_cols, block_counts, weight, cotangent):
    fd, slab = features.shape
    width = weight.shape[1]
    ranks = lax.axis_size("col")
    scalars = (block_cols.transpose(1, 2, 0), block_counts.transpose(1, 0))
    bf16, f32 = jnp.bfloat16, jnp.float32

    other = lax.ppermute(features, "row", SWAP)
    hbm = pl.BlockSpec(memory_space=pltpu.HBM)
    vmem = pl.BlockSpec(memory_space=pltpu.VMEM)
    smem = pl.BlockSpec(memory_space=pltpu.SMEM)
    a_blocks, part = pl.pallas_call(
        first_kernel,
        in_specs=[hbm] * 4,
        out_specs=[vmem, vmem],
        out_shape=[
            jax.ShapeDtypeStruct(a_blocks.shape, bf16),
            jax.ShapeDtypeStruct((fd, slab), f32),
        ],
        scratch_shapes=[
            pltpu.VMEM(features.shape, bf16),
            pltpu.SMEM(scalars[0].shape, jnp.int32),
            pltpu.SMEM(scalars[1].shape, jnp.int32),
            pltpu.SemaphoreType.DMA((3 + CHUNKS,)),
        ],
        compiler_params=pltpu.CompilerParams(vmem_limit_bytes=VMEM_LIMIT),
        name="first",
    )(*(pltpu.with_memory_space_constraint(x, pltpu.HBM) for x in (*scalars, features, a_blocks)))
    (msg,) = call(
        second_kernel,
        "second",
        scalars,
        (other, a_blocks, part, weight, cotangent),
        [((ranks, fd, 128 + width), bf16)],
    )
    msg = lax.all_to_all(msg.reshape(ranks * fd, 128 + width), "col", 0, 0, tiled=True)
    (back,) = call(dense_kernel, "dense", (), (msg,), [(msg.shape, bf16)])
    back = lax.all_to_all(back, "col", 0, 0, tiled=True).reshape(ranks, fd, 128 + width)
    send, dagg = call(
        send_kernel,
        "send",
        scalars,
        (back, a_blocks),
        [((fd, slab + width), f32), ((fd, slab), bf16)],
    )
    got = lax.ppermute(send, "row", SWAP)
    output, own = call(
        keep_kernel,
        "keep",
        scalars,
        (back, a_blocks, dagg),
        [((fd, slab), bf16), ((fd, slab), f32)],
    )
    scale = 1.0 / (slab * lax.axis_size("row")) ** 0.5
    grad_features, grad_weight = call(
        functools.partial(merge_kernel, scale),
        "merge",
        (),
        (own, send, got),
        [((fd, slab), bf16), ((fd, width), f32)],
    )
    return output, grad_weight, grad_features


def solution(mesh):
    placed = (
        P("col", "row"),
        P("row", None, None, None, None),
        P("row", None, None),
        P("row", None),
        P("col", None),
        P("col", "row"),
    )
    return jax.shard_map(
        local,
        mesh=mesh,
        in_specs=placed,
        out_specs=(P("col", "row"), P("col", None), P("col", "row")),
        check_vma=False,
    )
```

```python
import functools

import jax
import jax.numpy as jnp
from jax import lax
from jax.experimental import pallas as pl
from jax.experimental.pallas import tpu as pltpu
from jax.sharding import PartitionSpec as P

SWAP = [(0, 1), (1, 0)]
VMEM_LIMIT = 4 << 20
CHUNKS = 4
LANE = 128
ORDER_SEED = (
    29, 28, 24, 33, 35, 60, 23, 40, 11, 27, 61, 3, 5, 7, 42, 45,
    12, 59, 0, 55, 1, 44, 41, 14, 15, 17, 47, 20, 63, 10, 62, 54,
    36, 51, 21, 4, 43, 52, 9, 38, 34, 58, 39, 6, 46, 18, 8, 57,
    13, 37, 22, 30, 19, 53, 50, 25, 31, 32, 16, 2, 26, 56, 48, 49,
)


def order(ranks):
    listed = [d for d in ORDER_SEED if d < ranks]
    slots = [0] * ranks
    for slot, device in enumerate(listed):
        slots[device] = slot
    return listed, slots


def exchange(message):
    listed, _ = order(lax.axis_size("col"))
    return lax.all_to_all(message, "col", 0, 0, tiled=True, axis_index_groups=[listed])


def upper(shape):
    return lax.broadcasted_iota(jnp.int32, shape, len(shape) - 2) % 8 < 4


def swap_rows(x):
    tiles = x.reshape(x.shape[0] // 8, 8, x.shape[1])
    return pltpu.roll(tiles, 4, 1).reshape(x.shape)


def live_column(table, s, k, b):
    entry = table[s, k, b]
    return entry >= 0, pl.multiple_of(jnp.maximum(entry, 0), LANE)


def aggregate(table, feats, a_ref, s, b):
    total = jnp.zeros((8, LANE), jnp.float32)
    for k in range(2):
        live, col = live_column(table, s, k, b)
        x = feats[:, pl.ds(col, LANE)]
        x = lax.select(live, x, jnp.zeros_like(x))
        total += lax.dot_general(
            x, a_ref[b, s, k], (((1,), (1,)), ((), ())), preferred_element_type=jnp.float32
        )
    return total


def spread(table, dagg, a_ref, s, b, terms):
    for k in range(2):
        live, col = live_column(table, s, k, b)
        term = jnp.dot(dagg, a_ref[b, s, k], preferred_element_type=jnp.float32)
        term = lax.select(live, term, jnp.zeros_like(term))
        terms[:, pl.ds(col, LANE)] += term


def first_kernel(cols_hbm, counts_hbm, own_hbm, a_hbm, table, a_ref, total, own, cols, counts, sems):
    row = lax.axis_index("row")
    blocks = a_ref.shape[0]
    per = blocks // CHUNKS
    small = [
        pltpu.make_async_copy(src, dst, sems.at[i])
        for i, (src, dst) in enumerate(((cols_hbm, cols), (counts_hbm, counts), (own_hbm, own)))
    ]
    large = []
    for s in (row, 1 - row):
        for c in range(CHUNKS):
            here = pl.ds(c * per, per)
            large.append(
                pltpu.make_async_copy(
                    a_hbm.at[here, s], a_ref.at[here, s], sems.at[len(small) + len(large)]
                )
            )
    for copy in small + large:
        copy.start()
    for copy in small:
        copy.wait()
    for s in range(2):
        for b in range(blocks):
            for k in range(2):
                table[s, k, b] = jnp.where(k < counts[s, b], cols[s, k, b] * LANE, -1)
    for b in range(blocks):
        if b % per == 0:
            large[b // per].wait()
        total[:, b * LANE : (b + 1) * LANE] = aggregate(table, own, a_ref, row, b)
    for copy in large[CHUNKS:]:
        copy.wait()


def second_kernel(slots, table, other, a_ref, part, weight, cot, msg):
    row = lax.axis_index("row")
    half = weight.shape[1] // 2
    low = weight[:, :half].astype(jnp.float32)
    high = weight[:, half:].astype(jnp.float32)
    mask = upper(low.shape)
    w = (
        jnp.where(mask, low, swap_rows(high)).astype(jnp.bfloat16),
        jnp.where(mask, swap_rows(low), high).astype(jnp.bfloat16),
    )
    for b in range(a_ref.shape[0]):
        here = slice(b * LANE, (b + 1) * LANE)
        total = part[:, here] + aggregate(table, other, a_ref, 1 - row, b)
        total = total.astype(jnp.bfloat16)
        c = cot[:, here]
        c = (c, swap_rows(c.astype(jnp.float32)).astype(jnp.bfloat16))
        for q in range(2):
            slot = slots[2 * b + q]
            msg[slot, :, :LANE] = total
            msg[slot, :, LANE : 2 * LANE] = c[q]
            msg[slot, :, 2 * LANE :] = w[q]


def dense_kernel(slots, msg, back):
    half = len(slots) // 2
    tiles = [msg[8 * slot : 8 * slot + 8, :LANE].astype(jnp.float32) for slot in slots]
    agg = jnp.concatenate(
        [jnp.concatenate(tiles[:half], 0), jnp.concatenate(tiles[half:], 0)], 1
    ).astype(jnp.bfloat16)
    w = msg[:, 2 * LANE :]
    pre = jnp.dot(w, agg, preferred_element_type=jnp.float32)
    pre = pre[:, :LANE] + swap_rows(pre[:, LANE:])
    cot = msg[:, LANE : 2 * LANE].astype(jnp.float32)
    sig = jax.nn.sigmoid(pre)
    back[:, LANE : 2 * LANE] = (pre * sig).astype(jnp.bfloat16)
    dpre = cot * sig * (1.0 + pre * (1.0 - sig))
    dpre = jnp.where(upper(dpre.shape), dpre, 0.0)
    dpre = jnp.concatenate([dpre, swap_rows(dpre)], 1).astype(jnp.bfloat16)
    dagg = lax.dot_general(w, dpre, (((0,), (0,)), ((), ())), preferred_element_type=jnp.float32)
    for device, slot in enumerate(slots):
        rows = (device % half) * 8
        lanes = (device // half) * LANE
        back[8 * slot : 8 * slot + 8, :LANE] = dagg[rows : rows + 8, lanes : lanes + LANE].astype(
            jnp.bfloat16
        )
    grad = lax.dot_general(dpre, agg, (((1,), (1,)), ((), ())), preferred_element_type=jnp.float32)
    back[:, 2 * LANE :] = grad.astype(jnp.bfloat16)


def send_kernel(slots, table, back, a_ref, send, dagg_ref):
    row = lax.axis_index("row")
    blocks = a_ref.shape[0]
    slab = blocks * LANE
    half = (send.shape[1] - slab) // 2
    send[...] = jnp.zeros_like(send)
    grads = [jnp.zeros((8, half), jnp.float32) for _ in range(2)]
    for b in range(blocks):
        dagg = jnp.zeros((8, LANE), jnp.float32)
        for q in range(2):
            tile = back.at[slots[2 * b + q]]
            dagg += tile[:, :LANE].astype(jnp.float32)
            grads[q] += tile[:, 2 * LANE :].astype(jnp.float32)
        dagg = dagg.astype(jnp.bfloat16)
        dagg_ref[:, b * LANE : (b + 1) * LANE] = dagg
        spread(table, dagg, a_ref, 1 - row, b, send)
    mask = upper((8, half))
    send[:, slab : slab + half] = jnp.where(mask, grads[0], swap_rows(grads[1]))
    send[:, slab + half :] = jnp.where(mask, swap_rows(grads[0]), grads[1])


def keep_kernel(slots, table, back, a_ref, dagg_ref, out_hbm, own, out, sem):
    row = lax.axis_index("row")
    blocks = a_ref.shape[0]
    mask = upper((8, LANE))
    for b in range(blocks):
        first, second = (
            back[slots[2 * b + q], :, LANE : 2 * LANE].astype(jnp.float32) for q in range(2)
        )
        out[:, b * LANE : (b + 1) * LANE] = jnp.where(mask, first, swap_rows(second)).astype(
            jnp.bfloat16
        )
    copy = pltpu.make_async_copy(out, out_hbm, sem)
    copy.start()
    own[...] = jnp.zeros_like(own)
    for b in range(blocks):
        spread(table, dagg_ref[:, b * LANE : (b + 1) * LANE], a_ref, row, b, own)
    copy.wait()


def merge_kernel(scale, own, sent, got, grad_features, grad_weight):
    slab = own.shape[1]
    grad_features[...] = (own[...] + got[:, :slab]).astype(jnp.bfloat16)
    grad_weight[...] = (sent[:, slab:] + got[:, slab:]) * scale


HBM, VMEM, SMEM = (pl.BlockSpec(memory_space=m) for m in (pltpu.HBM, pltpu.VMEM, pltpu.SMEM))


def call(kernel, name, operands, outs, scratch=()):
    return pl.pallas_call(
        kernel,
        in_specs=[space for space, _ in operands],
        out_specs=[space for space, _, _ in outs],
        out_shape=[jax.ShapeDtypeStruct(shape, dtype) for _, shape, dtype in outs],
        scratch_shapes=list(scratch),
        compiler_params=pltpu.CompilerParams(vmem_limit_bytes=VMEM_LIMIT),
        name=name,
    )(*(array for _, array in operands))


def local(features, a_blocks, block_cols, block_counts, weight, cotangent):
    fd, slab = features.shape
    width = weight.shape[1]
    lanes = 2 * LANE + width // 2
    ranks = lax.axis_size("col")
    slots = order(ranks)[1]
    cols, counts = block_cols.transpose(1, 2, 0), block_counts.transpose(1, 0)
    bf16, f32, i32 = jnp.bfloat16, jnp.float32, jnp.int32

    other = lax.ppermute(features, "row", SWAP)
    table, blocks, part = call(
        first_kernel,
        "first",
        [
            (HBM, pltpu.with_memory_space_constraint(x, pltpu.HBM))
            for x in (cols, counts, features, a_blocks)
        ],
        [(SMEM, cols.shape, i32), (VMEM, a_blocks.shape, bf16), (VMEM, (fd, slab), f32)],
        [
            pltpu.VMEM(features.shape, bf16),
            pltpu.SMEM(cols.shape, i32),
            pltpu.SMEM(counts.shape, i32),
            pltpu.SemaphoreType.DMA((3 + 2 * CHUNKS,)),
        ],
    )
    (msg,) = call(
        functools.partial(second_kernel, slots),
        "second",
        [(SMEM, table)] + [(VMEM, x) for x in (other, blocks, part, weight, cotangent)],
        [(VMEM, (ranks, fd, lanes), bf16)],
    )
    msg = exchange(msg.reshape(ranks * fd, lanes))
    (back,) = call(
        functools.partial(dense_kernel, slots), "dense", [(VMEM, msg)], [(VMEM, msg.shape, bf16)]
    )
    back = exchange(back).reshape(ranks, fd, lanes)
    send, dagg = call(
        functools.partial(send_kernel, slots),
        "send",
        [(SMEM, table), (VMEM, back), (VMEM, blocks)],
        [(VMEM, (fd, slab + width), f32), (VMEM, (fd, slab), bf16)],
    )
    got = lax.ppermute(send, "row", SWAP)
    output, own = call(
        functools.partial(keep_kernel, slots),
        "keep",
        [(SMEM, table), (VMEM, back), (VMEM, blocks), (VMEM, dagg)],
        [(HBM, (fd, slab), bf16), (VMEM, (fd, slab), f32)],
        [pltpu.VMEM((fd, slab), bf16), pltpu.SemaphoreType.DMA],
    )
    scale = 1.0 / (slab * lax.axis_size("row")) ** 0.5
    grad_features, grad_weight = call(
        functools.partial(merge_kernel, scale),
        "merge",
        [(VMEM, own), (VMEM, send), (VMEM, got)],
        [(VMEM, (fd, slab), bf16), (VMEM, (fd, width), f32)],
    )
    return output, grad_weight, grad_features


def solution(mesh):
    placed = (
        P("col", "row"),
        P("row", None, None, None, None),
        P("row", None, None),
        P("row", None),
        P("col", None),
        P("col", "row"),
    )
    return jax.shard_map(
        local,
        mesh=mesh,
        in_specs=placed,
        out_specs=(P("col", "row"), P("col", None), P("col", "row")),
        check_vma=False,
    )
```

```python
import functools

import jax
import jax.numpy as jnp
from jax import lax
from jax.experimental import pallas as pl
from jax.experimental.pallas import tpu as pltpu
from jax.sharding import PartitionSpec as P

SWAP = [(0, 1), (1, 0)]
VMEM_LIMIT = 4 << 20
CHUNKS = 4
LANE = 128
ORDER_SEED = (
    29, 28, 24, 33, 35, 60, 23, 40, 11, 27, 61, 3, 5, 7, 42, 45,
    12, 59, 0, 55, 1, 44, 41, 14, 15, 17, 47, 20, 63, 10, 62, 54,
    36, 51, 21, 4, 43, 52, 9, 38, 34, 58, 39, 6, 46, 18, 8, 57,
    13, 37, 22, 30, 19, 53, 50, 25, 31, 32, 16, 2, 26, 56, 48, 49,
)


def order(ranks):
    listed = [d for d in ORDER_SEED if d < ranks]
    slots = [0] * ranks
    for slot, device in enumerate(listed):
        slots[device] = slot
    return listed, slots


def exchange(message):
    listed, _ = order(lax.axis_size("col"))
    return lax.all_to_all(message, "col", 0, 0, tiled=True, axis_index_groups=[listed])


def upper(shape):
    return lax.broadcasted_iota(jnp.int32, shape, len(shape) - 2) % 8 < 4


def swap_rows(x):
    tiles = x.reshape(x.shape[0] // 8, 8, x.shape[1])
    return pltpu.roll(tiles, 4, 1).reshape(x.shape)


def aggregate(table, feats, a_ref, s, b):
    return lax.dot_general(
        jnp.concatenate([feats[:, column(table, s, k, b)] for k in range(2)], 1),
        jnp.concatenate([a_ref[b, s, k] for k in range(2)], 1),
        (((1,), (1,)), ((), ())),
        preferred_element_type=jnp.float32,
    )


def spread(table, dagg, a_ref, s, b, terms):
    both = jnp.dot(
        dagg,
        jnp.concatenate([a_ref[b, s, k] for k in range(2)], 1),
        preferred_element_type=jnp.float32,
    )
    for k in range(2):
        terms[:, column(table, s, k, b)] += both[:, k * LANE : (k + 1) * LANE]


def column(table, s, k, b):
    return pl.ds(pl.multiple_of(table[s, k, b], LANE), LANE)


def first_kernel(
    cols_hbm, counts_hbm, own_hbm, a_hbm, table, a_ref, total, own, cols, counts, scalars, sems
):
    row = lax.axis_index("row")
    blocks = a_ref.shape[0]
    slab = total.shape[1]
    per = blocks // CHUNKS
    small = [
        pltpu.make_async_copy(src, dst, sems.at[i])
        for i, (src, dst) in enumerate(
            ((cols_hbm, cols), (counts_hbm, counts), (own_hbm, own.at[:, pl.ds(0, slab)]))
        )
    ]
    large = []
    for s in (row, 1 - row):
        for c in range(CHUNKS):
            here = pl.ds(c * per, per)
            large.append(
                pltpu.make_async_copy(
                    a_hbm.at[here, s], a_ref.at[here, s], sems.at[len(small) + len(large)]
                )
            )
    for copy in small + large:
        copy.start()
    own[:, slab:] = jnp.zeros((8, LANE), own.dtype)
    small[0].wait()
    small[1].wait()
    for s in range(2):
        live = lax.broadcasted_iota(jnp.int32, cols.shape[1:], 0) < counts[s : s + 1]
        table[s] = jnp.where(live, cols[s] * LANE, slab)
    listed = pltpu.make_async_copy(table, scalars, sems.at[0])
    listed.start()
    listed.wait()
    small[2].wait()
    for b in range(blocks):
        if b % per == 0:
            large[b // per].wait()
        total[:, b * LANE : (b + 1) * LANE] = aggregate(scalars, own, a_ref, row, b)
    for copy in large[CHUNKS:]:
        copy.wait()


def second_kernel(slots, table, other, a_ref, part, weight, cot, msg, feats):
    row = lax.axis_index("row")
    slab = other.shape[1]
    feats[:, :slab] = other[...]
    feats[:, slab:] = jnp.zeros((8, LANE), feats.dtype)
    half = weight.shape[1] // 2
    low = weight[:, :half].astype(jnp.float32)
    high = weight[:, half:].astype(jnp.float32)
    mask = upper(low.shape)
    w = (
        jnp.where(mask, low, swap_rows(high)).astype(jnp.bfloat16),
        jnp.where(mask, swap_rows(low), high).astype(jnp.bfloat16),
    )
    for b in range(a_ref.shape[0]):
        here = slice(b * LANE, (b + 1) * LANE)
        total = part[:, here] + aggregate(table, feats, a_ref, 1 - row, b)
        total = total.astype(jnp.bfloat16)
        c = cot[:, here]
        c = (c, swap_rows(c.astype(jnp.float32)).astype(jnp.bfloat16))
        for q in range(2):
            slot = slots[2 * b + q]
            msg[slot, :, :LANE] = total
            msg[slot, :, LANE : 2 * LANE] = c[q]
            msg[slot, :, 2 * LANE :] = w[q]


def dense_kernel(slots, msg, back):
    half = len(slots) // 2
    tiles = [msg[8 * slot : 8 * slot + 8, :LANE].astype(jnp.float32) for slot in slots]
    agg = jnp.concatenate(
        [jnp.concatenate(tiles[:half], 0), jnp.concatenate(tiles[half:], 0)], 1
    ).astype(jnp.bfloat16)
    w = msg[:, 2 * LANE :]
    pre = jnp.dot(w, agg, preferred_element_type=jnp.float32)
    pre = pre[:, :LANE] + swap_rows(pre[:, LANE:])
    cot = msg[:, LANE : 2 * LANE].astype(jnp.float32)
    sig = jax.nn.sigmoid(pre)
    back[:, LANE : 2 * LANE] = (pre * sig).astype(jnp.bfloat16)
    dpre = cot * sig * (1.0 + pre * (1.0 - sig))
    dpre = jnp.where(upper(dpre.shape), dpre, 0.0)
    dpre = jnp.concatenate([dpre, swap_rows(dpre)], 1).astype(jnp.bfloat16)
    dagg = lax.dot_general(w, dpre, (((0,), (0,)), ((), ())), preferred_element_type=jnp.float32)
    for device, slot in enumerate(slots):
        rows = (device % half) * 8
        lanes = (device // half) * LANE
        back[8 * slot : 8 * slot + 8, :LANE] = dagg[rows : rows + 8, lanes : lanes + LANE].astype(
            jnp.bfloat16
        )
    grad = lax.dot_general(dpre, agg, (((1,), (1,)), ((), ())), preferred_element_type=jnp.float32)
    back[:, 2 * LANE :] = grad.astype(jnp.bfloat16)


def send_kernel(slots, table, back, a_ref, send, dagg_ref):
    row = lax.axis_index("row")
    blocks = a_ref.shape[0]
    slab = blocks * LANE
    half = (send.shape[1] - slab) // 2
    send[...] = jnp.zeros_like(send)
    grads = [jnp.zeros((8, half), jnp.float32) for _ in range(2)]
    for b in range(blocks):
        dagg = jnp.zeros((8, LANE), jnp.float32)
        for q in range(2):
            tile = back.at[slots[2 * b + q]]
            dagg += tile[:, :LANE].astype(jnp.float32)
            grads[q] += tile[:, 2 * LANE :].astype(jnp.float32)
        dagg = dagg.astype(jnp.bfloat16)
        dagg_ref[:, b * LANE : (b + 1) * LANE] = dagg
        spread(table, dagg, a_ref, 1 - row, b, send)
    mask = upper((8, half))
    send[:, slab : slab + half] = jnp.where(mask, grads[0], swap_rows(grads[1]))
    send[:, slab + half :] = jnp.where(mask, swap_rows(grads[0]), grads[1])


def keep_kernel(slots, table, back, a_ref, dagg_ref, out_hbm, own, out, sem):
    row = lax.axis_index("row")
    blocks = a_ref.shape[0]
    mask = upper((8, LANE))
    for b in range(blocks):
        first, second = (
            back[slots[2 * b + q], :, LANE : 2 * LANE].astype(jnp.float32) for q in range(2)
        )
        out[:, b * LANE : (b + 1) * LANE] = jnp.where(mask, first, swap_rows(second)).astype(
            jnp.bfloat16
        )
    copy = pltpu.make_async_copy(out, out_hbm, sem)
    copy.start()
    own[...] = jnp.zeros_like(own)
    for b in range(blocks):
        spread(table, dagg_ref[:, b * LANE : (b + 1) * LANE], a_ref, row, b, own)
    copy.wait()


def merge_kernel(scale, own, sent, got, grad_features, grad_weight):
    slab = grad_features.shape[1]
    grad_features[...] = (own[:, :slab] + got[:, :slab]).astype(jnp.bfloat16)
    grad_weight[...] = (sent[:, slab:] + got[:, slab:]) * scale


HBM, VMEM, SMEM = (pl.BlockSpec(memory_space=m) for m in (pltpu.HBM, pltpu.VMEM, pltpu.SMEM))


def call(kernel, name, operands, outs, scratch=()):
    return pl.pallas_call(
        kernel,
        in_specs=[space for space, _ in operands],
        out_specs=[space for space, _, _ in outs],
        out_shape=[jax.ShapeDtypeStruct(shape, dtype) for _, shape, dtype in outs],
        scratch_shapes=list(scratch),
        compiler_params=pltpu.CompilerParams(vmem_limit_bytes=VMEM_LIMIT),
        name=name,
    )(*(array for _, array in operands))


def local(features, a_blocks, block_cols, block_counts, weight, cotangent):
    fd, slab = features.shape
    width = weight.shape[1]
    lanes = 2 * LANE + width // 2
    ranks = lax.axis_size("col")
    slots = order(ranks)[1]
    cols, counts = block_cols.transpose(1, 2, 0), block_counts.transpose(1, 0)
    bf16, f32, i32 = jnp.bfloat16, jnp.float32, jnp.int32

    other = lax.ppermute(features, "row", SWAP)
    table, blocks, part = call(
        first_kernel,
        "first",
        [
            (HBM, pltpu.with_memory_space_constraint(x, pltpu.HBM))
            for x in (cols, counts, features, a_blocks)
        ],
        [(VMEM, cols.shape, i32), (VMEM, a_blocks.shape, bf16), (VMEM, (fd, slab), f32)],
        [
            pltpu.VMEM((fd, slab + LANE), bf16),
            pltpu.VMEM(cols.shape, i32),
            pltpu.VMEM(counts.shape, i32),
            pltpu.SMEM(cols.shape, i32),
            pltpu.SemaphoreType.DMA((3 + 2 * CHUNKS,)),
        ],
    )
    (msg,) = call(
        functools.partial(second_kernel, slots),
        "second",
        [(SMEM, table)] + [(VMEM, x) for x in (other, blocks, part, weight, cotangent)],
        [(VMEM, (ranks, fd, lanes), bf16)],
        [pltpu.VMEM((fd, slab + LANE), bf16)],
    )
    msg = exchange(msg.reshape(ranks * fd, lanes))
    (back,) = call(
        functools.partial(dense_kernel, slots), "dense", [(VMEM, msg)], [(VMEM, msg.shape, bf16)]
    )
    back = exchange(back).reshape(ranks, fd, lanes)
    send, dagg = call(
        functools.partial(send_kernel, slots),
        "send",
        [(SMEM, table), (VMEM, back), (VMEM, blocks)],
        [(VMEM, (fd, slab + width), f32), (VMEM, (fd, slab), bf16)],
    )
    got = lax.ppermute(send, "row", SWAP)
    output, own = call(
        functools.partial(keep_kernel, slots),
        "keep",
        [(SMEM, table), (VMEM, back), (VMEM, blocks), (VMEM, dagg)],
        [(HBM, (fd, slab), bf16), (VMEM, (fd, slab + LANE), f32)],
        [pltpu.VMEM((fd, slab), bf16), pltpu.SemaphoreType.DMA],
    )
    scale = 1.0 / (slab * lax.axis_size("row")) ** 0.5
    grad_features, grad_weight = call(
        functools.partial(merge_kernel, scale),
        "merge",
        [(VMEM, own), (VMEM, send), (VMEM, got)],
        [(VMEM, (fd, slab), bf16), (VMEM, (fd, width), f32)],
    )
    return output, grad_weight, grad_features


def solution(mesh):
    placed = (
        P("col", "row"),
        P("row", None, None, None, None),
        P("row", None, None),
        P("row", None),
        P("col", None),
        P("col", "row"),
    )
    return jax.shard_map(
        local,
        mesh=mesh,
        in_specs=placed,
        out_specs=(P("col", "row"), P("col", None), P("col", "row")),
        check_vma=False,
    )
```

```python
import functools

import jax
import jax.numpy as jnp
from jax import lax
from jax.experimental import pallas as pl
from jax.experimental.pallas import tpu as pltpu
from jax.sharding import PartitionSpec as P

SWAP = [(0, 1), (1, 0)]
VMEM_LIMIT = 4 << 20
CHUNKS = 4
LANE = 128
ORDER_SEED = (
    29, 28, 24, 33, 35, 60, 23, 40, 11, 27, 61, 3, 5, 7, 42, 45,
    12, 59, 0, 55, 1, 44, 41, 14, 15, 17, 47, 20, 63, 10, 62, 54,
    36, 51, 21, 4, 43, 52, 9, 38, 34, 58, 39, 6, 46, 18, 8, 57,
    13, 37, 22, 30, 19, 53, 50, 25, 31, 32, 16, 2, 26, 56, 48, 49,
)


def order(ranks):
    listed = [d for d in ORDER_SEED if d < ranks]
    slots = [0] * ranks
    for slot, device in enumerate(listed):
        slots[device] = slot
    return listed, slots


def exchange(message):
    listed, _ = order(lax.axis_size("col"))
    return lax.all_to_all(message, "col", 0, 0, tiled=True, axis_index_groups=[listed])


def upper(shape):
    return lax.broadcasted_iota(jnp.int32, shape, len(shape) - 2) % 8 < 4


def swap_rows(x):
    tiles = x.reshape(x.shape[0] // 8, 8, x.shape[1])
    return pltpu.roll(tiles, 4, 1).reshape(x.shape)


def aggregate(picked, a_ref, s, b):
    return lax.dot_general(
        jnp.concatenate(picked, 1),
        jnp.concatenate([a_ref[b, s, k] for k in range(2)], 1),
        (((1,), (1,)), ((), ())),
        preferred_element_type=jnp.float32,
    )


def spread(table, dagg, a_ref, s, b, terms):
    both = jnp.dot(
        dagg,
        jnp.concatenate([a_ref[b, s, k] for k in range(2)], 1),
        preferred_element_type=jnp.float32,
    )
    for k in range(2):
        terms[:, column(table, s, k, b)] += both[:, k * LANE : (k + 1) * LANE]


def column(table, s, k, b):
    return pl.ds(pl.multiple_of(table[s, k * (table.shape[1] // 2) + b, 0], LANE), LANE)


def first_kernel(
    cols_hbm, counts_hbm, own_hbm, a_hbm, columns, a_ref, total, own, cols, counts, table, scalars, sems
):
    row = lax.axis_index("row")
    blocks = a_ref.shape[0]
    slab = total.shape[1]
    per = blocks // CHUNKS
    small = [
        pltpu.make_async_copy(src, dst, sems.at[i])
        for i, (src, dst) in enumerate(
            ((cols_hbm, cols), (counts_hbm, counts), (own_hbm, own.at[:, pl.ds(0, slab)]))
        )
    ]
    large = []
    for s in (row, 1 - row):
        for c in range(CHUNKS):
            here = pl.ds(c * per, per)
            large.append(
                pltpu.make_async_copy(
                    a_hbm.at[here, s], a_ref.at[here, s], sems.at[len(small) + len(large)]
                )
            )
    for copy in small + large:
        copy.start()
    own[:, slab:] = jnp.zeros((8, LANE), own.dtype)
    small[0].wait()
    small[1].wait()
    for s in range(2):
        live = lax.broadcasted_iota(jnp.int32, cols.shape[1:], 0) < counts[s : s + 1]
        table[s] = jnp.where(live, cols[s] * LANE, slab)
    listed = pltpu.make_async_copy(table, scalars, sems.at[0])
    listed.start()
    listed.wait()
    small[2].wait()
    for b in range(blocks):
        if b % per == 0:
            large[b // per].wait()
        picked = [
            own[:, pl.ds(pl.multiple_of(scalars[row, k, b], LANE), LANE)] for k in range(2)
        ]
        total[:, b * LANE : (b + 1) * LANE] = aggregate(picked, a_ref, row, b)
    for s in range(2):
        for k in range(2):
            for b in range(blocks):
                columns[s, k * blocks + b, :] = jnp.full((LANE,), scalars[s, k, b], jnp.int32)
    for copy in large[CHUNKS:]:
        copy.wait()


def second_kernel(slots, table, other, a_ref, part, weight, cot, msg, feats):
    row = lax.axis_index("row")
    slab = other.shape[1]
    feats[:, :slab] = other[...]
    feats[:, slab:] = jnp.zeros((8, LANE), feats.dtype)
    half = weight.shape[1] // 2
    low = weight[:, :half].astype(jnp.float32)
    high = weight[:, half:].astype(jnp.float32)
    mask = upper(low.shape)
    w = (
        jnp.where(mask, low, swap_rows(high)).astype(jnp.bfloat16),
        jnp.where(mask, swap_rows(low), high).astype(jnp.bfloat16),
    )
    for b in range(a_ref.shape[0]):
        here = slice(b * LANE, (b + 1) * LANE)
        picked = [feats[:, column(table, 1 - row, k, b)] for k in range(2)]
        total = part[:, here] + aggregate(picked, a_ref, 1 - row, b)
        total = total.astype(jnp.bfloat16)
        c = cot[:, here]
        c = (c, swap_rows(c.astype(jnp.float32)).astype(jnp.bfloat16))
        for q in range(2):
            slot = slots[2 * b + q]
            msg[slot, :, :LANE] = total
            msg[slot, :, LANE : 2 * LANE] = c[q]
            msg[slot, :, 2 * LANE :] = w[q]


def dense_kernel(slots, msg, back):
    half = len(slots) // 2
    tiles = [msg[8 * slot : 8 * slot + 8, :LANE].astype(jnp.float32) for slot in slots]
    agg = jnp.concatenate(
        [jnp.concatenate(tiles[:half], 0), jnp.concatenate(tiles[half:], 0)], 1
    ).astype(jnp.bfloat16)
    w = msg[:, 2 * LANE :]
    pre = jnp.dot(w, agg, preferred_element_type=jnp.float32)
    pre = pre[:, :LANE] + swap_rows(pre[:, LANE:])
    cot = msg[:, LANE : 2 * LANE].astype(jnp.float32)
    sig = jax.nn.sigmoid(pre)
    back[:, LANE : 2 * LANE] = (pre * sig).astype(jnp.bfloat16)
    dpre = cot * sig * (1.0 + pre * (1.0 - sig))
    dpre = jnp.where(upper(dpre.shape), dpre, 0.0)
    dpre = jnp.concatenate([dpre, swap_rows(dpre)], 1).astype(jnp.bfloat16)
    dagg = lax.dot_general(w, dpre, (((0,), (0,)), ((), ())), preferred_element_type=jnp.float32)
    for device, slot in enumerate(slots):
        rows = (device % half) * 8
        lanes = (device // half) * LANE
        back[8 * slot : 8 * slot + 8, :LANE] = dagg[rows : rows + 8, lanes : lanes + LANE].astype(
            jnp.bfloat16
        )
    grad = lax.dot_general(dpre, agg, (((1,), (1,)), ((), ())), preferred_element_type=jnp.float32)
    back[:, 2 * LANE :] = grad.astype(jnp.bfloat16)


def send_kernel(slots, table, back, a_ref, send, dagg_ref):
    row = lax.axis_index("row")
    blocks = a_ref.shape[0]
    slab = blocks * LANE
    half = (send.shape[1] - slab) // 2
    send[...] = jnp.zeros_like(send)
    grads = [jnp.zeros((8, half), jnp.float32) for _ in range(2)]
    for b in range(blocks):
        dagg = jnp.zeros((8, LANE), jnp.float32)
        for q in range(2):
            tile = back.at[slots[2 * b + q]]
            dagg += tile[:, :LANE].astype(jnp.float32)
            grads[q] += tile[:, 2 * LANE :].astype(jnp.float32)
        dagg = dagg.astype(jnp.bfloat16)
        dagg_ref[:, b * LANE : (b + 1) * LANE] = dagg
        spread(table, dagg, a_ref, 1 - row, b, send)
    mask = upper((8, half))
    send[:, slab : slab + half] = jnp.where(mask, grads[0], swap_rows(grads[1]))
    send[:, slab + half :] = jnp.where(mask, swap_rows(grads[0]), grads[1])


def keep_kernel(table, a_ref, dagg_ref, own):
    row = lax.axis_index("row")
    blocks = a_ref.shape[0]
    own[...] = jnp.zeros_like(own)
    for b in range(blocks):
        spread(table, dagg_ref[:, b * LANE : (b + 1) * LANE], a_ref, row, b, own)


def merge_kernel(slots, scale, back, own, sent, got, out, grad_features, grad_weight):
    mask = upper((8, LANE))
    for b in range(len(slots) // 2):
        first, second = (
            back[slots[2 * b + q], :, LANE : 2 * LANE].astype(jnp.float32) for q in range(2)
        )
        out[:, b * LANE : (b + 1) * LANE] = jnp.where(mask, first, swap_rows(second)).astype(
            jnp.bfloat16
        )
    slab = grad_features.shape[1]
    grad_features[...] = (own[:, :slab] + got[:, :slab]).astype(jnp.bfloat16)
    grad_weight[...] = (sent[:, slab:] + got[:, slab:]) * scale


HBM, VMEM = (pl.BlockSpec(memory_space=m) for m in (pltpu.HBM, pltpu.VMEM))


def call(kernel, name, operands, outs, scratch=()):
    return pl.pallas_call(
        kernel,
        in_specs=[space for space, _ in operands],
        out_specs=[space for space, _, _ in outs],
        out_shape=[jax.ShapeDtypeStruct(shape, dtype) for _, shape, dtype in outs],
        scratch_shapes=list(scratch),
        compiler_params=pltpu.CompilerParams(vmem_limit_bytes=VMEM_LIMIT),
        name=name,
    )(*(array for _, array in operands))


def local(features, a_blocks, block_cols, block_counts, weight, cotangent):
    fd, slab = features.shape
    width = weight.shape[1]
    lanes = 2 * LANE + width // 2
    ranks = lax.axis_size("col")
    slots = order(ranks)[1]
    cols, counts = block_cols.transpose(1, 2, 0), block_counts.transpose(1, 0)
    bf16, f32, i32 = jnp.bfloat16, jnp.float32, jnp.int32

    other = lax.ppermute(features, "row", SWAP)
    table, blocks, part = call(
        first_kernel,
        "first",
        [
            (HBM, pltpu.with_memory_space_constraint(x, pltpu.HBM))
            for x in (cols, counts, features, a_blocks)
        ],
        [
            (VMEM, (2, 2 * cols.shape[2], LANE), i32),
            (VMEM, a_blocks.shape, bf16),
            (VMEM, (fd, slab), f32),
        ],
        [
            pltpu.VMEM((fd, slab + LANE), bf16),
            pltpu.VMEM(cols.shape, i32),
            pltpu.VMEM(counts.shape, i32),
            pltpu.VMEM(cols.shape, i32),
            pltpu.SMEM(cols.shape, i32),
            pltpu.SemaphoreType.DMA((3 + 2 * CHUNKS,)),
        ],
    )
    (msg,) = call(
        functools.partial(second_kernel, slots),
        "second",
        [(VMEM, table)] + [(VMEM, x) for x in (other, blocks, part, weight, cotangent)],
        [(VMEM, (ranks, fd, lanes), bf16)],
        [pltpu.VMEM((fd, slab + LANE), bf16)],
    )
    msg = exchange(msg.reshape(ranks * fd, lanes))
    (back,) = call(
        functools.partial(dense_kernel, slots), "dense", [(VMEM, msg)], [(VMEM, msg.shape, bf16)]
    )
    back = exchange(back).reshape(ranks, fd, lanes)
    send, dagg = call(
        functools.partial(send_kernel, slots),
        "send",
        [(VMEM, table), (VMEM, back), (VMEM, blocks)],
        [(VMEM, (fd, slab + width), f32), (VMEM, (fd, slab), bf16)],
    )
    got = lax.ppermute(send, "row", SWAP)
    (own,) = call(
        keep_kernel,
        "keep",
        [(VMEM, table), (VMEM, blocks), (VMEM, dagg)],
        [(VMEM, (fd, slab + LANE), f32)],
    )
    scale = 1.0 / (slab * lax.axis_size("row")) ** 0.5
    output, grad_features, grad_weight = call(
        functools.partial(merge_kernel, slots, scale),
        "merge",
        [(VMEM, back), (VMEM, own), (VMEM, send), (VMEM, got)],
        [(VMEM, (fd, slab), bf16), (VMEM, (fd, slab), bf16), (VMEM, (fd, width), f32)],
    )
    return output, grad_weight, grad_features


def solution(mesh):
    placed = (
        P("col", "row"),
        P("row", None, None, None, None),
        P("row", None, None),
        P("row", None),
        P("col", None),
        P("col", "row"),
    )
    return jax.shard_map(
        local,
        mesh=mesh,
        in_specs=placed,
        out_specs=(P("col", "row"), P("col", None), P("col", "row")),
        check_vma=False,
    )
```

```python
import functools

import jax
import jax.numpy as jnp
from jax import lax
from jax.experimental import pallas as pl
from jax.experimental.pallas import tpu as pltpu
from jax.sharding import PartitionSpec as P

SWAP = [(0, 1), (1, 0)]
VMEM_LIMIT = 4 << 20
CHUNKS = 4
LANE = 128
ORDER_SEED = (
    58, 10, 56, 63, 55, 48, 4, 54, 34, 0, 3, 5, 27, 44, 50, 33,
    14, 62, 30, 19, 42, 60, 12, 28, 24, 37, 61, 36, 47, 35, 45, 7,
    8, 6, 41, 22, 51, 57, 46, 15, 39, 16, 52, 59, 49, 1, 13, 38,
    31, 53, 2, 11, 20, 40, 29, 9, 17, 26, 21, 25, 23, 32, 18, 43,
)


def order(ranks):
    listed = [d for d in ORDER_SEED if d < ranks]
    slots = [0] * ranks
    for slot, device in enumerate(listed):
        slots[device] = slot
    return listed, slots


def exchange(message):
    listed, _ = order(lax.axis_size("col"))
    return lax.all_to_all(message, "col", 0, 0, tiled=True, axis_index_groups=[listed])


def upper(shape):
    return lax.broadcasted_iota(jnp.int32, shape, len(shape) - 2) % 8 < 4


def swap_rows(x):
    tiles = x.reshape(x.shape[0] // 8, 8, x.shape[1])
    return pltpu.roll(tiles, 4, 1).reshape(x.shape)


def aggregate(picked, a_ref, s, b):
    return lax.dot_general(
        jnp.concatenate(picked, 1),
        jnp.concatenate([a_ref[b, s, k] for k in range(2)], 1),
        (((1,), (1,)), ((), ())),
        preferred_element_type=jnp.float32,
    )


def spread(table, dagg, a_ref, s, b, terms):
    both = jnp.dot(
        dagg,
        jnp.concatenate([a_ref[b, s, k] for k in range(2)], 1),
        preferred_element_type=jnp.float32,
    )
    for k in range(2):
        terms[:, column(table, s, k, b)] += both[:, k * LANE : (k + 1) * LANE]


def column(table, s, k, b):
    return pl.ds(pl.multiple_of(table[s, k * (table.shape[1] // 2) + b, 0], LANE), LANE)


def first_kernel(
    cols_hbm, counts_hbm, own_hbm, a_hbm, columns, a_ref, total, own, cols, counts, table, scalars, sems
):
    row = lax.axis_index("row")
    blocks = a_ref.shape[0]
    slab = total.shape[1]
    per = blocks // CHUNKS
    small = [
        pltpu.make_async_copy(src, dst, sems.at[i])
        for i, (src, dst) in enumerate(
            ((cols_hbm, cols), (counts_hbm, counts), (own_hbm, own.at[:, pl.ds(0, slab)]))
        )
    ]
    large = []
    for s in (row, 1 - row):
        for c in range(CHUNKS):
            here = pl.ds(c * per, per)
            large.append(
                pltpu.make_async_copy(
                    a_hbm.at[here, s], a_ref.at[here, s], sems.at[len(small) + len(large)]
                )
            )
    for copy in small + large:
        copy.start()
    own[:, slab:] = jnp.zeros((8, LANE), own.dtype)
    small[0].wait()
    small[1].wait()
    for s in range(2):
        live = lax.broadcasted_iota(jnp.int32, cols.shape[1:], 0) < counts[s : s + 1]
        table[s] = jnp.where(live, cols[s] * LANE, slab)
    listed = pltpu.make_async_copy(table, scalars, sems.at[0])
    listed.start()
    listed.wait()
    small[2].wait()
    for b in range(blocks):
        if b % per == 0:
            large[b // per].wait()
        picked = [
            own[:, pl.ds(pl.multiple_of(scalars[row, k, b], LANE), LANE)] for k in range(2)
        ]
        total[:, b * LANE : (b + 1) * LANE] = aggregate(picked, a_ref, row, b)
    for s in range(2):
        for k in range(2):
            for b in range(blocks):
                columns[s, k * blocks + b, :] = jnp.full((LANE,), scalars[s, k, b], jnp.int32)
    for copy in large[CHUNKS:]:
        copy.wait()


def second_kernel(slots, table, other, a_ref, part, weight, cot, msg, feats):
    row = lax.axis_index("row")
    slab = other.shape[1]
    feats[:, :slab] = other[...]
    feats[:, slab:] = jnp.zeros((8, LANE), feats.dtype)
    half = weight.shape[1] // 2
    low = weight[:, :half].astype(jnp.float32)
    high = weight[:, half:].astype(jnp.float32)
    mask = upper(low.shape)
    w = (
        jnp.where(mask, low, swap_rows(high)).astype(jnp.bfloat16),
        jnp.where(mask, swap_rows(low), high).astype(jnp.bfloat16),
    )
    for b in range(a_ref.shape[0]):
        here = slice(b * LANE, (b + 1) * LANE)
        picked = [feats[:, column(table, 1 - row, k, b)] for k in range(2)]
        total = part[:, here] + aggregate(picked, a_ref, 1 - row, b)
        total = total.astype(jnp.bfloat16)
        c = cot[:, here]
        c = (c, swap_rows(c.astype(jnp.float32)).astype(jnp.bfloat16))
        for q in range(2):
            slot = slots[2 * b + q]
            msg[slot, :, :LANE] = total
            msg[slot, :, LANE : 2 * LANE] = c[q]
            msg[slot, :, 2 * LANE :] = w[q]


def dense_kernel(slots, msg, back):
    half = len(slots) // 2
    tiles = [msg[8 * slot : 8 * slot + 8, :LANE].astype(jnp.float32) for slot in slots]
    agg = jnp.concatenate(
        [jnp.concatenate(tiles[:half], 0), jnp.concatenate(tiles[half:], 0)], 1
    ).astype(jnp.bfloat16)
    w = msg[:, 2 * LANE :]
    pre = jnp.dot(w, agg, preferred_element_type=jnp.float32)
    pre = pre[:, :LANE] + swap_rows(pre[:, LANE:])
    cot = msg[:, LANE : 2 * LANE].astype(jnp.float32)
    sig = jax.nn.sigmoid(pre)
    back[:, LANE : 2 * LANE] = (pre * sig).astype(jnp.bfloat16)
    dpre = cot * sig * (1.0 + pre * (1.0 - sig))
    dpre = jnp.where(upper(dpre.shape), dpre, 0.0)
    dpre = jnp.concatenate([dpre, swap_rows(dpre)], 1).astype(jnp.bfloat16)
    dagg = lax.dot_general(w, dpre, (((0,), (0,)), ((), ())), preferred_element_type=jnp.float32)
    for device, slot in enumerate(slots):
        rows = (device % half) * 8
        lanes = (device // half) * LANE
        back[8 * slot : 8 * slot + 8, :LANE] = dagg[rows : rows + 8, lanes : lanes + LANE].astype(
            jnp.bfloat16
        )
    grad = lax.dot_general(dpre, agg, (((1,), (1,)), ((), ())), preferred_element_type=jnp.float32)
    back[:, 2 * LANE :] = grad.astype(jnp.bfloat16)


def send_kernel(slots, table, back, a_ref, send, dagg_ref):
    row = lax.axis_index("row")
    blocks = a_ref.shape[0]
    slab = blocks * LANE
    half = (send.shape[1] - slab) // 2
    send[...] = jnp.zeros_like(send)
    grads = [jnp.zeros((8, half), jnp.float32) for _ in range(2)]
    for b in range(blocks):
        dagg = jnp.zeros((8, LANE), jnp.float32)
        for q in range(2):
            tile = back.at[slots[2 * b + q]]
            dagg += tile[:, :LANE].astype(jnp.float32)
            grads[q] += tile[:, 2 * LANE :].astype(jnp.float32)
        dagg = dagg.astype(jnp.bfloat16)
        dagg_ref[:, b * LANE : (b + 1) * LANE] = dagg
        spread(table, dagg, a_ref, 1 - row, b, send)
    mask = upper((8, half))
    send[:, slab : slab + half] = jnp.where(mask, grads[0], swap_rows(grads[1]))
    send[:, slab + half :] = jnp.where(mask, swap_rows(grads[0]), grads[1])


def keep_kernel(table, a_ref, dagg_ref, own):
    row = lax.axis_index("row")
    blocks = a_ref.shape[0]
    own[...] = jnp.zeros_like(own)
    for b in range(blocks):
        spread(table, dagg_ref[:, b * LANE : (b + 1) * LANE], a_ref, row, b, own)


def merge_kernel(slots, scale, back, own, sent, got, out, grad_features, grad_weight):
    mask = upper((8, LANE))
    for b in range(len(slots) // 2):
        first, second = (
            back[slots[2 * b + q], :, LANE : 2 * LANE].astype(jnp.float32) for q in range(2)
        )
        out[:, b * LANE : (b + 1) * LANE] = jnp.where(mask, first, swap_rows(second)).astype(
            jnp.bfloat16
        )
    slab = grad_features.shape[1]
    grad_features[...] = (own[:, :slab] + got[:, :slab]).astype(jnp.bfloat16)
    grad_weight[...] = (sent[:, slab:] + got[:, slab:]) * scale


HBM, VMEM = (pl.BlockSpec(memory_space=m) for m in (pltpu.HBM, pltpu.VMEM))


def call(kernel, name, operands, outs, scratch=()):
    return pl.pallas_call(
        kernel,
        in_specs=[space for space, _ in operands],
        out_specs=[space for space, _, _ in outs],
        out_shape=[jax.ShapeDtypeStruct(shape, dtype) for _, shape, dtype in outs],
        scratch_shapes=list(scratch),
        compiler_params=pltpu.CompilerParams(vmem_limit_bytes=VMEM_LIMIT),
        name=name,
    )(*(array for _, array in operands))


def local(features, a_blocks, block_cols, block_counts, weight, cotangent):
    fd, slab = features.shape
    width = weight.shape[1]
    lanes = 2 * LANE + width // 2
    ranks = lax.axis_size("col")
    slots = order(ranks)[1]
    cols, counts = block_cols.transpose(1, 2, 0), block_counts.transpose(1, 0)
    bf16, f32, i32 = jnp.bfloat16, jnp.float32, jnp.int32

    other = lax.ppermute(features, "row", SWAP)
    table, blocks, part = call(
        first_kernel,
        "first",
        [
            (HBM, pltpu.with_memory_space_constraint(x, pltpu.HBM))
            for x in (cols, counts, features, a_blocks)
        ],
        [
            (VMEM, (2, 2 * cols.shape[2], LANE), i32),
            (VMEM, a_blocks.shape, bf16),
            (VMEM, (fd, slab), f32),
        ],
        [
            pltpu.VMEM((fd, slab + LANE), bf16),
            pltpu.VMEM(cols.shape, i32),
            pltpu.VMEM(counts.shape, i32),
            pltpu.VMEM(cols.shape, i32),
            pltpu.SMEM(cols.shape, i32),
            pltpu.SemaphoreType.DMA((3 + 2 * CHUNKS,)),
        ],
    )
    (msg,) = call(
        functools.partial(second_kernel, slots),
        "second",
        [(VMEM, table)] + [(VMEM, x) for x in (other, blocks, part, weight, cotangent)],
        [(VMEM, (ranks, fd, lanes), bf16)],
        [pltpu.VMEM((fd, slab + LANE), bf16)],
    )
    msg = exchange(msg.reshape(ranks * fd, lanes))
    (back,) = call(
        functools.partial(dense_kernel, slots), "dense", [(VMEM, msg)], [(VMEM, msg.shape, bf16)]
    )
    back = exchange(back).reshape(ranks, fd, lanes)
    send, dagg = call(
        functools.partial(send_kernel, slots),
        "send",
        [(VMEM, table), (VMEM, back), (VMEM, blocks)],
        [(VMEM, (fd, slab + width), f32), (VMEM, (fd, slab), bf16)],
    )
    got = lax.ppermute(send, "row", SWAP)
    (own,) = call(
        keep_kernel,
        "keep",
        [(VMEM, table), (VMEM, blocks), (VMEM, dagg)],
        [(VMEM, (fd, slab + LANE), f32)],
    )
    scale = 1.0 / (slab * lax.axis_size("row")) ** 0.5
    output, grad_features, grad_weight = call(
        functools.partial(merge_kernel, slots, scale),
        "merge",
        [(VMEM, back), (VMEM, own), (VMEM, send), (VMEM, got)],
        [(VMEM, (fd, slab), bf16), (VMEM, (fd, slab), bf16), (VMEM, (fd, width), f32)],
    )
    return output, grad_weight, grad_features


def solution(mesh):
    placed = (
        P("col", "row"),
        P("row", None, None, None, None),
        P("row", None, None),
        P("row", None),
        P("col", None),
        P("col", "row"),
    )
    return jax.shard_map(
        local,
        mesh=mesh,
        in_specs=placed,
        out_specs=(P("col", "row"), P("col", None), P("col", "row")),
        check_vma=False,
    )
```

```python
import functools

import jax
import jax.numpy as jnp
from jax import lax
from jax.experimental import pallas as pl
from jax.experimental.pallas import tpu as pltpu
from jax.sharding import PartitionSpec as P

SWAP = [(0, 1), (1, 0)]
VMEM_LIMIT = 4 << 20
CHUNKS = 4
LANE = 128
ORDER_SEED = (
    58, 10, 56, 63, 55, 48, 4, 54, 34, 0, 3, 5, 27, 44, 50, 33,
    14, 62, 30, 19, 42, 60, 12, 28, 24, 37, 61, 36, 47, 35, 45, 7,
    8, 6, 41, 22, 51, 57, 46, 15, 39, 16, 52, 59, 49, 1, 13, 38,
    31, 53, 2, 11, 20, 40, 29, 9, 17, 26, 21, 25, 23, 32, 18, 43,
)


def order(ranks):
    listed = [d for d in ORDER_SEED if d < ranks]
    slots = [0] * ranks
    for slot, device in enumerate(listed):
        slots[device] = slot
    return listed, slots


def exchange(message):
    listed, _ = order(lax.axis_size("col"))
    return lax.all_to_all(message, "col", 0, 0, tiled=True, axis_index_groups=[listed])


def aggregate(picked, a_ref, s, b):
    return lax.dot_general(
        jnp.concatenate(picked, 1),
        jnp.concatenate([a_ref[b, s, k] for k in range(2)], 1),
        (((1,), (1,)), ((), ())),
        preferred_element_type=jnp.float32,
    )


def spread(table, dagg, a_ref, s, b, terms):
    both = jnp.dot(
        dagg,
        jnp.concatenate([a_ref[b, s, k] for k in range(2)], 1),
        preferred_element_type=jnp.float32,
    )
    for k in range(2):
        terms[:, column(table, s, k, b)] += both[:, k * LANE : (k + 1) * LANE]


def column(table, s, k, b):
    return pl.ds(pl.multiple_of(table[s, k * (table.shape[1] // 2) + b, 0], LANE), LANE)


def first_kernel(
    cols_hbm, counts_hbm, own_hbm, a_hbm, columns, a_ref, total, own, cols, counts, table, scalars, sems
):
    row = lax.axis_index("row")
    blocks = a_ref.shape[0]
    slab = total.shape[1]
    per = blocks // CHUNKS
    small = [
        pltpu.make_async_copy(src, dst, sems.at[i])
        for i, (src, dst) in enumerate(
            ((cols_hbm, cols), (counts_hbm, counts), (own_hbm, own.at[:, pl.ds(0, slab)]))
        )
    ]
    large = []
    for s in (row, 1 - row):
        for c in range(CHUNKS):
            here = pl.ds(c * per, per)
            large.append(
                pltpu.make_async_copy(
                    a_hbm.at[here, s], a_ref.at[here, s], sems.at[len(small) + len(large)]
                )
            )
    for copy in small + large:
        copy.start()
    own[:, slab:] = jnp.zeros((8, LANE), own.dtype)
    small[0].wait()
    small[1].wait()
    for s in range(2):
        live = lax.broadcasted_iota(jnp.int32, cols.shape[1:], 0) < counts[s : s + 1]
        table[s] = jnp.where(live, cols[s] * LANE, slab)
    listed = pltpu.make_async_copy(table, scalars, sems.at[0])
    listed.start()
    listed.wait()
    small[2].wait()
    for b in range(blocks):
        if b % per == 0:
            large[b // per].wait()
        picked = [
            own[:, pl.ds(pl.multiple_of(scalars[row, k, b], LANE), LANE)] for k in range(2)
        ]
        total[:, b * LANE : (b + 1) * LANE] = aggregate(picked, a_ref, row, b)
    for s in range(2):
        for k in range(2):
            for b in range(blocks):
                columns[s, k * blocks + b, :] = jnp.full((LANE,), scalars[s, k, b], jnp.int32)
    for copy in large[CHUNKS:]:
        copy.wait()


def second_kernel(slots, table, other, a_ref, part, weight, cot, msg, feats):
    row = lax.axis_index("row")
    slab = other.shape[1]
    feats[:, :slab] = other[...]
    feats[:, slab:] = jnp.zeros((8, LANE), feats.dtype)
    w = two(weight[...])
    for b in range(a_ref.shape[0]):
        here = slice(b * LANE, (b + 1) * LANE)
        picked = [feats[:, column(table, 1 - row, k, b)] for k in range(2)]
        low, high = two(part[:, here] + aggregate(picked, a_ref, 1 - row, b))
        c = two(cot[:, here])
        for q in range(2):
            slot = slots[2 * b + q]
            msg[slot, :, :LANE] = low
            msg[slot, :, LANE : 2 * LANE] = high
            msg[slot, :, 2 * LANE : 3 * LANE] = c[q]
            msg[slot, :, 3 * LANE :] = w[q]


def two(x):
    x = x.astype(jnp.float32)
    return x[:4].astype(jnp.bfloat16), x[4:].astype(jnp.bfloat16)


def rows(x):
    return x.astype(jnp.float32).reshape(-1, x.shape[-1])


def dense_kernel(slots, msg, back):
    agg = jnp.concatenate(
        [
            msg[slot, :, half * LANE : (half + 1) * LANE].astype(jnp.float32)
            for slot in slots
            for half in range(2)
        ],
        0,
    ).astype(jnp.bfloat16)
    w = rows(msg[:, :, 3 * LANE :]).astype(jnp.bfloat16)
    pre = jnp.dot(w, agg, preferred_element_type=jnp.float32)
    cot = rows(msg[:, :, 2 * LANE : 3 * LANE])
    sig = jax.nn.sigmoid(pre)
    tiles = (len(slots), 4, -1)
    back[:, :, 2 * LANE : 3 * LANE] = (pre * sig).reshape(tiles).astype(jnp.bfloat16)
    dpre = (cot * sig * (1.0 + pre * (1.0 - sig))).astype(jnp.bfloat16)
    dagg = lax.dot_general(w, dpre, (((0,), (0,)), ((), ())), preferred_element_type=jnp.float32)
    for device, slot in enumerate(slots):
        low, high = two(dagg[8 * device : 8 * device + 8])
        back[slot, :, :LANE] = low
        back[slot, :, LANE : 2 * LANE] = high
    grad = lax.dot_general(dpre, agg, (((1,), (1,)), ((), ())), preferred_element_type=jnp.float32)
    back[:, :, 3 * LANE :] = grad.reshape(tiles).astype(jnp.bfloat16)


def send_kernel(slots, table, back, a_ref, send, dagg_ref):
    row = lax.axis_index("row")
    blocks = a_ref.shape[0]
    slab = blocks * LANE
    send[...] = jnp.zeros_like(send)
    grads = [jnp.zeros((4, send.shape[1] - slab), jnp.float32) for _ in range(2)]
    for b in range(blocks):
        dagg = jnp.zeros((4, 2 * LANE), jnp.float32)
        for q in range(2):
            tile = back.at[slots[2 * b + q]]
            dagg += tile[:, : 2 * LANE].astype(jnp.float32)
            grads[q] += tile[:, 3 * LANE :].astype(jnp.float32)
        dagg = jnp.concatenate([dagg[:, :LANE], dagg[:, LANE:]], 0).astype(jnp.bfloat16)
        dagg_ref[:, b * LANE : (b + 1) * LANE] = dagg
        spread(table, dagg, a_ref, 1 - row, b, send)
    send[:, slab:] = jnp.concatenate(grads, 0)


def keep_kernel(table, a_ref, dagg_ref, own):
    row = lax.axis_index("row")
    blocks = a_ref.shape[0]
    own[...] = jnp.zeros_like(own)
    for b in range(blocks):
        spread(table, dagg_ref[:, b * LANE : (b + 1) * LANE], a_ref, row, b, own)


def merge_kernel(slots, scale, back, own, sent, got, out, grad_features, grad_weight):
    for b in range(len(slots) // 2):
        tiles = [
            back[slots[2 * b + q], :, 2 * LANE : 3 * LANE].astype(jnp.float32) for q in range(2)
        ]
        out[:, b * LANE : (b + 1) * LANE] = jnp.concatenate(tiles, 0).astype(jnp.bfloat16)
    slab = grad_features.shape[1]
    grad_features[...] = (own[:, :slab] + got[:, :slab]).astype(jnp.bfloat16)
    grad_weight[...] = (sent[:, slab:] + got[:, slab:]) * scale


HBM, VMEM = (pl.BlockSpec(memory_space=m) for m in (pltpu.HBM, pltpu.VMEM))


def call(kernel, name, operands, outs, scratch=()):
    return pl.pallas_call(
        kernel,
        in_specs=[space for space, _ in operands],
        out_specs=[space for space, _, _ in outs],
        out_shape=[jax.ShapeDtypeStruct(shape, dtype) for _, shape, dtype in outs],
        scratch_shapes=list(scratch),
        compiler_params=pltpu.CompilerParams(vmem_limit_bytes=VMEM_LIMIT),
        name=name,
    )(*(array for _, array in operands))


def local(features, a_blocks, block_cols, block_counts, weight, cotangent):
    fd, slab = features.shape
    width = weight.shape[1]
    lanes = 3 * LANE + width
    ranks = lax.axis_size("col")
    slots = order(ranks)[1]
    cols, counts = block_cols.transpose(1, 2, 0), block_counts.transpose(1, 0)
    bf16, f32, i32 = jnp.bfloat16, jnp.float32, jnp.int32

    other = lax.ppermute(features, "row", SWAP)
    table, blocks, part = call(
        first_kernel,
        "first",
        [
            (HBM, pltpu.with_memory_space_constraint(x, pltpu.HBM))
            for x in (cols, counts, features, a_blocks)
        ],
        [
            (VMEM, (2, 2 * cols.shape[2], LANE), i32),
            (VMEM, a_blocks.shape, bf16),
            (VMEM, (fd, slab), f32),
        ],
        [
            pltpu.VMEM((fd, slab + LANE), bf16),
            pltpu.VMEM(cols.shape, i32),
            pltpu.VMEM(counts.shape, i32),
            pltpu.VMEM(cols.shape, i32),
            pltpu.SMEM(cols.shape, i32),
            pltpu.SemaphoreType.DMA((3 + 2 * CHUNKS,)),
        ],
    )
    (msg,) = call(
        functools.partial(second_kernel, slots),
        "second",
        [(VMEM, table)] + [(VMEM, x) for x in (other, blocks, part, weight, cotangent)],
        [(VMEM, (ranks, fd // 2, lanes), bf16)],
        [pltpu.VMEM((fd, slab + LANE), bf16)],
    )
    msg = exchange(msg)
    (back,) = call(
        functools.partial(dense_kernel, slots), "dense", [(VMEM, msg)], [(VMEM, msg.shape, bf16)]
    )
    back = exchange(back)
    send, dagg = call(
        functools.partial(send_kernel, slots),
        "send",
        [(VMEM, table), (VMEM, back), (VMEM, blocks)],
        [(VMEM, (fd, slab + width), f32), (VMEM, (fd, slab), bf16)],
    )
    got = lax.ppermute(send, "row", SWAP)
    (own,) = call(
        keep_kernel,
        "keep",
        [(VMEM, table), (VMEM, blocks), (VMEM, dagg)],
        [(VMEM, (fd, slab + LANE), f32)],
    )
    scale = 1.0 / (slab * lax.axis_size("row")) ** 0.5
    output, grad_features, grad_weight = call(
        functools.partial(merge_kernel, slots, scale),
        "merge",
        [(VMEM, back), (VMEM, own), (VMEM, send), (VMEM, got)],
        [(VMEM, (fd, slab), bf16), (VMEM, (fd, slab), bf16), (VMEM, (fd, width), f32)],
    )
    return output, grad_weight, grad_features


def solution(mesh):
    placed = (
        P("col", "row"),
        P("row", None, None, None, None),
        P("row", None, None),
        P("row", None),
        P("col", None),
        P("col", "row"),
    )
    return jax.shard_map(
        local,
        mesh=mesh,
        in_specs=placed,
        out_specs=(P("col", "row"), P("col", None), P("col", "row")),
        check_vma=False,
    )
```

```python
import functools

import jax
import jax.numpy as jnp
from jax import lax
from jax.experimental import pallas as pl
from jax.experimental.pallas import tpu as pltpu
from jax.sharding import PartitionSpec as P

SWAP = [(0, 1), (1, 0)]
VMEM_LIMIT = 4 << 20
CHUNKS = 4
LANE = 128
BUFFERS = 2
ORDER_SEED = (
    58, 10, 56, 63, 55, 48, 4, 54, 34, 0, 3, 5, 27, 44, 50, 33,
    14, 62, 30, 19, 42, 60, 12, 28, 24, 37, 61, 36, 47, 35, 45, 7,
    8, 6, 41, 22, 51, 57, 46, 15, 39, 16, 52, 59, 49, 1, 13, 38,
    31, 53, 2, 11, 20, 40, 29, 9, 17, 26, 21, 25, 23, 32, 18, 43,
)


def order(ranks):
    listed = [d for d in ORDER_SEED if d < ranks]
    slots = [0] * ranks
    for slot, device in enumerate(listed):
        slots[device] = slot
    return listed, slots


def exchange(message):
    listed, _ = order(lax.axis_size("col"))
    return lax.all_to_all(message, "col", 0, 0, tiled=True, axis_index_groups=[listed])


def aggregate(picked, a_ref, s, b):
    return lax.dot_general(
        jnp.concatenate(picked, 1),
        jnp.concatenate([a_ref[b, s, k] for k in range(2)], 1),
        (((1,), (1,)), ((), ())),
        preferred_element_type=jnp.float32,
    )


def spread(table, dagg, a_ref, s, b, terms):
    both = jnp.dot(
        dagg,
        jnp.concatenate([a_ref[b, s, k] for k in range(2)], 1),
        preferred_element_type=jnp.float32,
    )
    for k in range(2):
        buffer = terms[(2 * b + k) % len(terms)]
        buffer[:, column(table, s, k, b)] += both[:, k * LANE : (k + 1) * LANE]


def column(table, s, k, b):
    return pl.ds(pl.multiple_of(table[s, k * (table.shape[1] // 2) + b, 0], LANE), LANE)


def first_kernel(
    slots,
    cols_hbm,
    counts_hbm,
    own_hbm,
    weight_hbm,
    cot_hbm,
    a_hbm,
    columns,
    a_ref,
    total,
    msg,
    own,
    weight,
    cot,
    cols,
    counts,
    table,
    scalars,
    sems,
):
    row = lax.axis_index("row")
    blocks = a_ref.shape[0]
    slab = total.shape[1]
    per = blocks // CHUNKS
    small = [
        pltpu.make_async_copy(src, dst, sems.at[i])
        for i, (src, dst) in enumerate(
            (
                (cols_hbm, cols),
                (counts_hbm, counts),
                (own_hbm, own.at[:, pl.ds(0, slab)]),
                (weight_hbm, weight),
                (cot_hbm, cot),
            )
        )
    ]
    large = []
    for s in (row, 1 - row):
        for c in range(CHUNKS):
            here = pl.ds(c * per, per)
            large.append(
                pltpu.make_async_copy(
                    a_hbm.at[here, s], a_ref.at[here, s], sems.at[len(small) + len(large)]
                )
            )
    for copy in small + large:
        copy.start()
    own[:, slab:] = jnp.zeros((8, LANE), own.dtype)
    small[0].wait()
    small[1].wait()
    for s in range(2):
        live = lax.broadcasted_iota(jnp.int32, cols.shape[1:], 0) < counts[s : s + 1]
        table[s] = jnp.where(live, cols[s] * LANE, slab)
    listed = pltpu.make_async_copy(table, scalars, sems.at[0])
    listed.start()
    listed.wait()
    small[2].wait()
    for b in range(blocks):
        if b % per == 0:
            large[b // per].wait()
        picked = [
            own[:, pl.ds(pl.multiple_of(scalars[row, k, b], LANE), LANE)] for k in range(2)
        ]
        total[:, b * LANE : (b + 1) * LANE] = aggregate(picked, a_ref, row, b)
    for s in range(2):
        for k in range(2):
            for b in range(blocks):
                columns[s, k * blocks + b, :] = jnp.full((LANE,), scalars[s, k, b], jnp.int32)
    small[3].wait()
    small[4].wait()
    w = two(weight[...])
    for b in range(blocks):
        c = two(cot[:, b * LANE : (b + 1) * LANE])
        for q in range(2):
            slot = slots[2 * b + q]
            msg[slot, :, 2 * LANE : 3 * LANE] = c[q]
            msg[slot, :, 3 * LANE :] = w[q]
    for copy in large[CHUNKS:]:
        copy.wait()


def second_kernel(slots, table, other, a_ref, part, begun, msg, feats):
    del begun
    row = lax.axis_index("row")
    slab = other.shape[1]
    feats[:, :slab] = other[...]
    feats[:, slab:] = jnp.zeros((8, LANE), feats.dtype)
    for b in range(a_ref.shape[0]):
        here = slice(b * LANE, (b + 1) * LANE)
        picked = [feats[:, column(table, 1 - row, k, b)] for k in range(2)]
        low, high = two(part[:, here] + aggregate(picked, a_ref, 1 - row, b))
        for q in range(2):
            slot = slots[2 * b + q]
            msg[slot, :, :LANE] = low
            msg[slot, :, LANE : 2 * LANE] = high


def two(x):
    x = x.astype(jnp.float32)
    return x[:4].astype(jnp.bfloat16), x[4:].astype(jnp.bfloat16)


def rows(x):
    return x.astype(jnp.float32).reshape(-1, x.shape[-1])


def dense_kernel(slots, msg, back):
    agg = jnp.concatenate(
        [
            msg[slot, :, half * LANE : (half + 1) * LANE].astype(jnp.float32)
            for slot in slots
            for half in range(2)
        ],
        0,
    ).astype(jnp.bfloat16)
    w = msg[:, :, 3 * LANE :].reshape(4 * len(slots), -1)
    pre = jnp.dot(w, agg, preferred_element_type=jnp.float32)
    cot = rows(msg[:, :, 2 * LANE : 3 * LANE])
    sig = jax.nn.sigmoid(pre)
    tiles = (len(slots), 4, -1)
    back[:, :, 2 * LANE : 3 * LANE] = (pre * sig).reshape(tiles).astype(jnp.bfloat16)
    dpre = (cot * sig * (1.0 + pre * (1.0 - sig))).astype(jnp.bfloat16)
    dagg = lax.dot_general(w, dpre, (((0,), (0,)), ((), ())), preferred_element_type=jnp.float32)
    for device, slot in enumerate(slots):
        low, high = two(dagg[8 * device : 8 * device + 8])
        back[slot, :, :LANE] = low
        back[slot, :, LANE : 2 * LANE] = high
    grad = lax.dot_general(dpre, agg, (((1,), (1,)), ((), ())), preferred_element_type=jnp.float32)
    back[:, :, 3 * LANE :] = grad.astype(jnp.bfloat16).reshape(tiles)


def send_kernel(slots, table, back, a_ref, send, dagg_ref, *more):
    row = lax.axis_index("row")
    blocks = a_ref.shape[0]
    slab = blocks * LANE
    for buffer in (send, *more):
        buffer[...] = jnp.zeros_like(buffer)
    grads = [jnp.zeros((4, send.shape[1] - slab), jnp.float32) for _ in range(2)]
    for b in range(blocks):
        dagg = jnp.zeros((4, 2 * LANE), jnp.float32)
        for q in range(2):
            tile = back.at[slots[2 * b + q]]
            dagg += tile[:, : 2 * LANE].astype(jnp.float32)
            grads[q] += tile[:, 3 * LANE :].astype(jnp.float32)
        dagg = jnp.concatenate([dagg[:, :LANE], dagg[:, LANE:]], 0).astype(jnp.bfloat16)
        dagg_ref[:, b * LANE : (b + 1) * LANE] = dagg
        spread(table, dagg, a_ref, 1 - row, b, (send, *more))
    total = send[:, :slab]
    for buffer in more:
        total += buffer[:, :slab]
    send[:, :slab] = total
    send[:, slab:] = jnp.concatenate(grads, 0)


def keep_kernel(table, a_ref, dagg_ref, *own):
    row = lax.axis_index("row")
    blocks = a_ref.shape[0]
    for buffer in own:
        buffer[...] = jnp.zeros_like(buffer)
    for b in range(blocks):
        spread(table, dagg_ref[:, b * LANE : (b + 1) * LANE], a_ref, row, b, own)


def merge_kernel(slots, scale, back, sent, got, *refs):
    own, (out, grad_features, grad_weight) = refs[:-3], refs[-3:]
    for b in range(len(slots) // 2):
        tiles = [
            back[slots[2 * b + q], :, 2 * LANE : 3 * LANE].astype(jnp.float32) for q in range(2)
        ]
        out[:, b * LANE : (b + 1) * LANE] = jnp.concatenate(tiles, 0).astype(jnp.bfloat16)
    slab = grad_features.shape[1]
    total = got[:, :slab]
    for buffer in own:
        total += buffer[:, :slab]
    grad_features[...] = total.astype(jnp.bfloat16)
    grad_weight[...] = (sent[:, slab:] + got[:, slab:]) * scale


HBM, VMEM = (pl.BlockSpec(memory_space=m) for m in (pltpu.HBM, pltpu.VMEM))


def call(kernel, name, operands, outs, scratch=(), aliases=None):
    return pl.pallas_call(
        kernel,
        in_specs=[space for space, _ in operands],
        out_specs=[space for space, _, _ in outs],
        out_shape=[jax.ShapeDtypeStruct(shape, dtype) for _, shape, dtype in outs],
        scratch_shapes=list(scratch),
        input_output_aliases=aliases or {},
        compiler_params=pltpu.CompilerParams(vmem_limit_bytes=VMEM_LIMIT),
        name=name,
    )(*(array for _, array in operands))


def local(features, a_blocks, block_cols, block_counts, weight, cotangent):
    fd, slab = features.shape
    width = weight.shape[1]
    lanes = 3 * LANE + width
    ranks = lax.axis_size("col")
    slots = order(ranks)[1]
    cols, counts = block_cols.transpose(1, 2, 0), block_counts.transpose(1, 0)
    bf16, f32, i32 = jnp.bfloat16, jnp.float32, jnp.int32

    other = lax.ppermute(features, "row", SWAP)
    table, blocks, part, msg = call(
        functools.partial(first_kernel, slots),
        "first",
        [
            (HBM, pltpu.with_memory_space_constraint(x, pltpu.HBM))
            for x in (cols, counts, features, weight, cotangent, a_blocks)
        ],
        [
            (VMEM, (2, 2 * cols.shape[2], LANE), i32),
            (VMEM, a_blocks.shape, bf16),
            (VMEM, (fd, slab), f32),
            (VMEM, (ranks, fd // 2, lanes), bf16),
        ],
        [
            pltpu.VMEM((fd, slab + LANE), bf16),
            pltpu.VMEM(weight.shape, bf16),
            pltpu.VMEM(cotangent.shape, bf16),
            pltpu.VMEM(cols.shape, i32),
            pltpu.VMEM(counts.shape, i32),
            pltpu.VMEM(cols.shape, i32),
            pltpu.SMEM(cols.shape, i32),
            pltpu.SemaphoreType.DMA((5 + 2 * CHUNKS,)),
        ],
    )
    (msg,) = call(
        functools.partial(second_kernel, slots),
        "second",
        [(VMEM, x) for x in (table, other, blocks, part, msg)],
        [(VMEM, (ranks, fd // 2, lanes), bf16)],
        [pltpu.VMEM((fd, slab + LANE), bf16)],
        {4: 0},
    )
    msg = exchange(msg)
    (back,) = call(
        functools.partial(dense_kernel, slots), "dense", [(VMEM, msg)], [(VMEM, msg.shape, bf16)]
    )
    back = exchange(back)
    send, dagg = call(
        functools.partial(send_kernel, slots),
        "send",
        [(VMEM, table), (VMEM, back), (VMEM, blocks)],
        [(VMEM, (fd, slab + width), f32), (VMEM, (fd, slab), bf16)],
        [pltpu.VMEM((fd, slab + LANE), f32)] * (BUFFERS - 1),
    )
    got = lax.ppermute(send, "row", SWAP)
    own = call(
        keep_kernel,
        "keep",
        [(VMEM, table), (VMEM, blocks), (VMEM, dagg)],
        [(VMEM, (fd, slab + LANE), f32)] * BUFFERS,
    )
    scale = 1.0 / (slab * lax.axis_size("row")) ** 0.5
    output, grad_features, grad_weight = call(
        functools.partial(merge_kernel, slots, scale),
        "merge",
        [(VMEM, x) for x in (back, send, got, *own)],
        [(VMEM, (fd, slab), bf16), (VMEM, (fd, slab), bf16), (VMEM, (fd, width), f32)],
    )
    return output, grad_weight, grad_features


def solution(mesh):
    placed = (
        P("col", "row"),
        P("row", None, None, None, None),
        P("row", None, None),
        P("row", None),
        P("col", None),
        P("col", "row"),
    )
    return jax.shard_map(
        local,
        mesh=mesh,
        in_specs=placed,
        out_specs=(P("col", "row"), P("col", None), P("col", "row")),
        check_vma=False,
    )
```

```python
import functools

import jax
import jax.numpy as jnp
from jax import lax
from jax.experimental import pallas as pl
from jax.experimental.pallas import tpu as pltpu
from jax.sharding import PartitionSpec as P

SWAP = [(0, 1), (1, 0)]
VMEM_LIMIT = 4 << 20
CHUNKS = 4
LANE = 128
BUFFERS = 2
ORDER_SEED = (
    58, 10, 56, 63, 55, 48, 4, 54, 34, 0, 3, 5, 27, 44, 50, 33,
    14, 62, 30, 19, 42, 60, 12, 28, 24, 37, 61, 36, 47, 35, 45, 7,
    8, 6, 41, 22, 51, 57, 46, 15, 39, 16, 52, 59, 49, 1, 13, 38,
    31, 53, 2, 11, 20, 40, 29, 9, 17, 26, 21, 25, 23, 32, 18, 43,
)


def order(ranks):
    listed = [d for d in ORDER_SEED if d < ranks]
    slots = [0] * ranks
    for slot, device in enumerate(listed):
        slots[device] = slot
    return listed, slots


def exchange(message):
    listed, _ = order(lax.axis_size("col"))
    return lax.all_to_all(message, "col", 0, 0, tiled=True, axis_index_groups=[listed])


def aggregate(picked, a_ref, s, b):
    return lax.dot_general(
        jnp.concatenate(picked, 1),
        jnp.concatenate([a_ref[b, s, k] for k in range(2)], 1),
        (((1,), (1,)), ((), ())),
        preferred_element_type=jnp.float32,
    )


def spread(table, dagg, a_ref, s, b, terms):
    both = jnp.dot(
        dagg,
        jnp.concatenate([a_ref[b, s, k] for k in range(2)], 1),
        preferred_element_type=jnp.float32,
    )
    for k in range(2):
        buffer = terms[(2 * b + k) % len(terms)]
        buffer[:, column(table, s, k, b)] += both[:, k * LANE : (k + 1) * LANE]


def column(table, s, k, b):
    return pl.ds(pl.multiple_of(table[s, k * (table.shape[1] // 2) + b, 0], LANE), LANE)


def first_kernel(
    slots,
    cols_hbm,
    counts_hbm,
    own_hbm,
    weight_hbm,
    cot_hbm,
    a_hbm,
    columns,
    a_ref,
    total,
    msg,
    own,
    weight,
    cot,
    cols,
    counts,
    table,
    scalars,
    sems,
):
    row = lax.axis_index("row")
    blocks = a_ref.shape[0]
    slab = total.shape[1]
    per = blocks // CHUNKS
    small = [
        pltpu.make_async_copy(src, dst, sems.at[i])
        for i, (src, dst) in enumerate(
            (
                (cols_hbm, cols),
                (counts_hbm, counts),
                (own_hbm, own.at[:, pl.ds(0, slab)]),
                (weight_hbm, weight),
                (cot_hbm, cot),
            )
        )
    ]
    large = []
    for s in (row, 1 - row):
        for c in range(CHUNKS):
            here = pl.ds(c * per, per)
            large.append(
                pltpu.make_async_copy(
                    a_hbm.at[here, s], a_ref.at[here, s], sems.at[len(small) + len(large)]
                )
            )
    for copy in small + large:
        copy.start()
    own[:, slab:] = jnp.zeros((8, LANE), own.dtype)
    small[0].wait()
    small[1].wait()
    for s in range(2):
        live = lax.broadcasted_iota(jnp.int32, cols.shape[1:], 0) < counts[s : s + 1]
        table[s] = jnp.where(live, cols[s] * LANE, slab)
    listed = pltpu.make_async_copy(table, scalars, sems.at[0])
    listed.start()
    listed.wait()
    small[2].wait()
    for b in range(blocks):
        if b % per == 0:
            large[b // per].wait()
        picked = [
            own[:, pl.ds(pl.multiple_of(scalars[row, k, b], LANE), LANE)] for k in range(2)
        ]
        total[:, b * LANE : (b + 1) * LANE] = aggregate(picked, a_ref, row, b)
    for s in range(2):
        for k in range(2):
            for b in range(blocks):
                columns[s, k * blocks + b, :] = jnp.full((LANE,), scalars[s, k, b], jnp.int32)
    small[3].wait()
    small[4].wait()
    w = two(weight[...])
    for b in range(blocks):
        c = two(cot[:, b * LANE : (b + 1) * LANE])
        for q in range(2):
            slot = slots[2 * b + q]
            msg[slot, :, 2 * LANE : 3 * LANE] = c[q]
            msg[slot, :, 3 * LANE :] = w[q]
    for copy in large[CHUNKS:]:
        copy.wait()


def second_kernel(slots, table, other, a_ref, part, begun, msg, feats):
    del begun
    row = lax.axis_index("row")
    slab = other.shape[1]
    feats[:, :slab] = other[...]
    feats[:, slab:] = jnp.zeros((8, LANE), feats.dtype)
    for b in range(a_ref.shape[0]):
        here = slice(b * LANE, (b + 1) * LANE)
        picked = [feats[:, column(table, 1 - row, k, b)] for k in range(2)]
        low, high = two(part[:, here] + aggregate(picked, a_ref, 1 - row, b))
        for q in range(2):
            slot = slots[2 * b + q]
            msg[slot, :, :LANE] = low
            msg[slot, :, LANE : 2 * LANE] = high


def two(x):
    x = x.astype(jnp.float32)
    return x[:4].astype(jnp.bfloat16), x[4:].astype(jnp.bfloat16)


def rows(x):
    return x.astype(jnp.float32).reshape(-1, x.shape[-1])


def dense_kernel(slots, msg, back):
    agg = jnp.concatenate(
        [
            msg[slot, :, half * LANE : (half + 1) * LANE].astype(jnp.float32)
            for slot in slots
            for half in range(2)
        ],
        0,
    ).astype(jnp.bfloat16)
    w = msg[:, :, 3 * LANE :].reshape(4 * len(slots), -1)
    pre = jnp.dot(w, agg, preferred_element_type=jnp.float32)
    cot = rows(msg[:, :, 2 * LANE : 3 * LANE])
    sig = jax.nn.sigmoid(pre)
    tiles = (len(slots), 4, -1)
    back[:, :, 2 * LANE : 3 * LANE] = (pre * sig).reshape(tiles).astype(jnp.bfloat16)
    dpre = (cot * sig * (1.0 + pre * (1.0 - sig))).astype(jnp.bfloat16)
    dagg = lax.dot_general(w, dpre, (((0,), (0,)), ((), ())), preferred_element_type=jnp.float32)
    for device, slot in enumerate(slots):
        low, high = two(dagg[8 * device : 8 * device + 8])
        back[slot, :, :LANE] = low
        back[slot, :, LANE : 2 * LANE] = high
    grad = lax.dot_general(dpre, agg, (((1,), (1,)), ((), ())), preferred_element_type=jnp.float32)
    back[:, :, 3 * LANE :] = grad.astype(jnp.bfloat16).reshape(tiles)


def send_kernel(slots, table, back, a_ref, send, dagg_ref, *more):
    row = lax.axis_index("row")
    blocks = a_ref.shape[0]
    slab = blocks * LANE
    for buffer in (send, *more):
        buffer[...] = jnp.zeros_like(buffer)
    grads = [jnp.zeros((4, send.shape[1] - slab), jnp.float32) for _ in range(2)]
    for b in range(blocks):
        dagg = jnp.zeros((4, 2 * LANE), jnp.float32)
        for q in range(2):
            tile = back.at[slots[2 * b + q]]
            dagg += tile[:, : 2 * LANE].astype(jnp.float32)
            grads[q] += tile[:, 3 * LANE :].astype(jnp.float32)
        dagg = jnp.concatenate([dagg[:, :LANE], dagg[:, LANE:]], 0).astype(jnp.bfloat16)
        dagg_ref[:, b * LANE : (b + 1) * LANE] = dagg
        spread(table, dagg, a_ref, 1 - row, b, (send, *more))
    total = send[:, :slab]
    for buffer in more:
        total += buffer[:, :slab]
    send[:, :slab] = total
    send[:, slab:] = jnp.concatenate(grads, 0)


def keep_kernel(slots, table, back, a_ref, dagg_ref, out_hbm, *refs):
    own, (out, sem) = refs[:-2], refs[-2:]
    row = lax.axis_index("row")
    for b in range(len(slots) // 2):
        tiles = [
            back[slots[2 * b + q], :, 2 * LANE : 3 * LANE].astype(jnp.float32) for q in range(2)
        ]
        out[:, b * LANE : (b + 1) * LANE] = jnp.concatenate(tiles, 0).astype(jnp.bfloat16)
    copy = pltpu.make_async_copy(out, out_hbm, sem)
    copy.start()
    blocks = a_ref.shape[0]
    for buffer in own:
        buffer[...] = jnp.zeros_like(buffer)
    for b in range(blocks):
        spread(table, dagg_ref[:, b * LANE : (b + 1) * LANE], a_ref, row, b, own)
    copy.wait()


def merge_kernel(scale, sent, got, *refs):
    own, (grad_features, grad_weight) = refs[:-2], refs[-2:]
    slab = grad_features.shape[1]
    total = got[:, :slab]
    for buffer in own:
        total += buffer[:, :slab]
    grad_features[...] = total.astype(jnp.bfloat16)
    grad_weight[...] = (sent[:, slab:] + got[:, slab:]) * scale


HBM, VMEM = (pl.BlockSpec(memory_space=m) for m in (pltpu.HBM, pltpu.VMEM))


def call(kernel, name, operands, outs, scratch=(), aliases=None):
    return pl.pallas_call(
        kernel,
        in_specs=[space for space, _ in operands],
        out_specs=[space for space, _, _ in outs],
        out_shape=[jax.ShapeDtypeStruct(shape, dtype) for _, shape, dtype in outs],
        scratch_shapes=list(scratch),
        input_output_aliases=aliases or {},
        compiler_params=pltpu.CompilerParams(vmem_limit_bytes=VMEM_LIMIT),
        name=name,
    )(*(array for _, array in operands))


def local(features, a_blocks, block_cols, block_counts, weight, cotangent):
    fd, slab = features.shape
    width = weight.shape[1]
    lanes = 3 * LANE + width
    ranks = lax.axis_size("col")
    slots = order(ranks)[1]
    cols, counts = block_cols.transpose(1, 2, 0), block_counts.transpose(1, 0)
    bf16, f32, i32 = jnp.bfloat16, jnp.float32, jnp.int32

    other = lax.ppermute(features, "row", SWAP)
    table, blocks, part, msg = call(
        functools.partial(first_kernel, slots),
        "first",
        [
            (HBM, pltpu.with_memory_space_constraint(x, pltpu.HBM))
            for x in (cols, counts, features, weight, cotangent, a_blocks)
        ],
        [
            (VMEM, (2, 2 * cols.shape[2], LANE), i32),
            (VMEM, a_blocks.shape, bf16),
            (VMEM, (fd, slab), f32),
            (VMEM, (ranks, fd // 2, lanes), bf16),
        ],
        [
            pltpu.VMEM((fd, slab + LANE), bf16),
            pltpu.VMEM(weight.shape, bf16),
            pltpu.VMEM(cotangent.shape, bf16),
            pltpu.VMEM(cols.shape, i32),
            pltpu.VMEM(counts.shape, i32),
            pltpu.VMEM(cols.shape, i32),
            pltpu.SMEM(cols.shape, i32),
            pltpu.SemaphoreType.DMA((5 + 2 * CHUNKS,)),
        ],
    )
    (msg,) = call(
        functools.partial(second_kernel, slots),
        "second",
        [(VMEM, x) for x in (table, other, blocks, part, msg)],
        [(VMEM, (ranks, fd // 2, lanes), bf16)],
        [pltpu.VMEM((fd, slab + LANE), bf16)],
        {4: 0},
    )
    msg = exchange(msg)
    (back,) = call(
        functools.partial(dense_kernel, slots), "dense", [(VMEM, msg)], [(VMEM, msg.shape, bf16)]
    )
    back = exchange(back)
    send, dagg = call(
        functools.partial(send_kernel, slots),
        "send",
        [(VMEM, table), (VMEM, back), (VMEM, blocks)],
        [(VMEM, (fd, slab + width), f32), (VMEM, (fd, slab), bf16)],
        [pltpu.VMEM((fd, slab + LANE), f32)] * (BUFFERS - 1),
    )
    got = lax.ppermute(send, "row", SWAP)
    output, *own = call(
        functools.partial(keep_kernel, slots),
        "keep",
        [(VMEM, x) for x in (table, back, blocks, dagg)],
        [(HBM, (fd, slab), bf16)] + [(VMEM, (fd, slab + LANE), f32)] * BUFFERS,
        [pltpu.VMEM((fd, slab), bf16), pltpu.SemaphoreType.DMA],
    )
    scale = 1.0 / (slab * lax.axis_size("row")) ** 0.5
    grad_features, grad_weight = call(
        functools.partial(merge_kernel, scale),
        "merge",
        [(VMEM, x) for x in (send, got, *own)],
        [(VMEM, (fd, slab), bf16), (VMEM, (fd, width), f32)],
    )
    return output, grad_weight, grad_features


def solution(mesh):
    placed = (
        P("col", "row"),
        P("row", None, None, None, None),
        P("row", None, None),
        P("row", None),
        P("col", None),
        P("col", "row"),
    )
    return jax.shard_map(
        local,
        mesh=mesh,
        in_specs=placed,
        out_specs=(P("col", "row"), P("col", None), P("col", "row")),
        check_vma=False,
    )
```

```python
import functools

import jax
import jax.numpy as jnp
from jax import lax
from jax.experimental import pallas as pl
from jax.experimental.pallas import tpu as pltpu
from jax.sharding import PartitionSpec as P

SWAP = [(0, 1), (1, 0)]
VMEM_LIMIT = 4 << 20
CHUNKS = 4
LANE = 128
BUFFERS = 2
ORDER_SEED = (
    58, 6, 0, 38, 4, 25, 16, 49, 13, 43, 10, 51, 34, 32, 56, 31,
    18, 37, 17, 30, 52, 45, 23, 33, 55, 5, 47, 26, 29, 35, 53, 54,
    7, 44, 27, 50, 2, 1, 41, 8, 19, 24, 12, 46, 22, 9, 21, 40,
    14, 39, 3, 28, 62, 59, 61, 57, 60, 48, 42, 36, 20, 63, 15, 11,
)


def order(ranks):
    listed = [d for d in ORDER_SEED if d < ranks]
    slots = [0] * ranks
    for slot, device in enumerate(listed):
        slots[device] = slot
    return listed, slots


def exchange(message):
    listed, _ = order(lax.axis_size("col"))
    return lax.all_to_all(message, "col", 0, 0, tiled=True, axis_index_groups=[listed])


def aggregate(picked, a_ref, s, b):
    return lax.dot_general(
        jnp.concatenate(picked, 1),
        jnp.concatenate([a_ref[b, s, k] for k in range(2)], 1),
        (((1,), (1,)), ((), ())),
        preferred_element_type=jnp.float32,
    )


def spread(table, dagg, a_ref, s, b, terms):
    both = jnp.dot(
        dagg,
        jnp.concatenate([a_ref[b, s, k] for k in range(2)], 1),
        preferred_element_type=jnp.float32,
    )
    for k in range(2):
        buffer = terms[(2 * b + k) % len(terms)]
        buffer[:, column(table, s, k, b)] += both[:, k * LANE : (k + 1) * LANE]


def column(table, s, k, b):
    return pl.ds(pl.multiple_of(table[s, k * (table.shape[1] // 2) + b, 0], LANE), LANE)


def first_kernel(
    slots,
    cols_hbm,
    counts_hbm,
    own_hbm,
    weight_hbm,
    cot_hbm,
    a_hbm,
    columns,
    a_ref,
    total,
    msg,
    own,
    weight,
    cot,
    cols,
    counts,
    table,
    scalars,
    sems,
):
    row = lax.axis_index("row")
    blocks = a_ref.shape[0]
    slab = total.shape[1]
    per = blocks // CHUNKS
    small = [
        pltpu.make_async_copy(src, dst, sems.at[i])
        for i, (src, dst) in enumerate(
            (
                (cols_hbm, cols),
                (counts_hbm, counts),
                (own_hbm, own.at[:, pl.ds(0, slab)]),
                (weight_hbm, weight),
                (cot_hbm, cot),
            )
        )
    ]
    large = []
    for s in (row, 1 - row):
        for c in range(CHUNKS):
            here = pl.ds(c * per, per)
            large.append(
                pltpu.make_async_copy(
                    a_hbm.at[here, s], a_ref.at[here, s], sems.at[len(small) + len(large)]
                )
            )
    for copy in small + large:
        copy.start()
    own[:, slab:] = jnp.zeros((8, LANE), own.dtype)
    small[0].wait()
    small[1].wait()
    for s in range(2):
        live = lax.broadcasted_iota(jnp.int32, cols.shape[1:], 0) < counts[s : s + 1]
        table[s] = jnp.where(live, cols[s] * LANE, slab)
    listed = pltpu.make_async_copy(table, scalars, sems.at[0])
    listed.start()
    listed.wait()
    small[2].wait()
    for b in range(blocks):
        if b % per == 0:
            large[b // per].wait()
        picked = [
            own[:, pl.ds(pl.multiple_of(scalars[row, k, b], LANE), LANE)] for k in range(2)
        ]
        total[:, b * LANE : (b + 1) * LANE] = aggregate(picked, a_ref, row, b)
    for s in range(2):
        for k in range(2):
            for b in range(blocks):
                columns[s, k * blocks + b, :] = jnp.full((LANE,), scalars[s, k, b], jnp.int32)
    small[3].wait()
    small[4].wait()
    w = two(weight[...])
    for b in range(blocks):
        c = two(cot[:, b * LANE : (b + 1) * LANE])
        for q in range(2):
            slot = slots[2 * b + q]
            msg[slot, :, 2 * LANE : 3 * LANE] = c[q]
            msg[slot, :, 3 * LANE :] = w[q]
    for copy in large[CHUNKS:]:
        copy.wait()


def second_kernel(slots, table, other, a_ref, part, begun, msg, feats):
    del begun
    row = lax.axis_index("row")
    slab = other.shape[1]
    feats[:, :slab] = other[...]
    feats[:, slab:] = jnp.zeros((8, LANE), feats.dtype)
    for b in range(a_ref.shape[0]):
        here = slice(b * LANE, (b + 1) * LANE)
        picked = [feats[:, column(table, 1 - row, k, b)] for k in range(2)]
        low, high = two(part[:, here] + aggregate(picked, a_ref, 1 - row, b))
        for q in range(2):
            slot = slots[2 * b + q]
            msg[slot, :, :LANE] = low
            msg[slot, :, LANE : 2 * LANE] = high


def two(x):
    x = x.astype(jnp.float32)
    return x[:4].astype(jnp.bfloat16), x[4:].astype(jnp.bfloat16)


def rows(x):
    return x.astype(jnp.float32).reshape(-1, x.shape[-1])


def dense_kernel(slots, msg, back):
    agg = jnp.concatenate(
        [
            msg[slot, :, half * LANE : (half + 1) * LANE].astype(jnp.float32)
            for slot in slots
            for half in range(2)
        ],
        0,
    ).astype(jnp.bfloat16)
    w = msg[:, :, 3 * LANE :].reshape(4 * len(slots), -1)
    pre = jnp.dot(w, agg, preferred_element_type=jnp.float32)
    cot = rows(msg[:, :, 2 * LANE : 3 * LANE])
    sig = jax.nn.sigmoid(pre)
    tiles = (len(slots), 4, -1)
    back[:, :, 2 * LANE : 3 * LANE] = (pre * sig).reshape(tiles).astype(jnp.bfloat16)
    dpre = (cot * sig * (1.0 + pre * (1.0 - sig))).astype(jnp.bfloat16)
    dagg = lax.dot_general(w, dpre, (((0,), (0,)), ((), ())), preferred_element_type=jnp.float32)
    for device, slot in enumerate(slots):
        low, high = two(dagg[8 * device : 8 * device + 8])
        back[slot, :, :LANE] = low
        back[slot, :, LANE : 2 * LANE] = high
    grad = lax.dot_general(dpre, agg, (((1,), (1,)), ((), ())), preferred_element_type=jnp.float32)
    back[:, :, 3 * LANE :] = grad.astype(jnp.bfloat16).reshape(tiles)


def send_kernel(slots, table, back, a_ref, send, dagg_ref, *more):
    row = lax.axis_index("row")
    blocks = a_ref.shape[0]
    slab = blocks * LANE
    for buffer in (send, *more):
        buffer[...] = jnp.zeros_like(buffer)
    grads = [jnp.zeros((4, send.shape[1] - slab), jnp.float32) for _ in range(2)]
    for b in range(blocks):
        dagg = jnp.zeros((4, 2 * LANE), jnp.float32)
        for q in range(2):
            tile = back.at[slots[2 * b + q]]
            dagg += tile[:, : 2 * LANE].astype(jnp.float32)
            grads[q] += tile[:, 3 * LANE :].astype(jnp.float32)
        dagg = jnp.concatenate([dagg[:, :LANE], dagg[:, LANE:]], 0).astype(jnp.bfloat16)
        dagg_ref[:, b * LANE : (b + 1) * LANE] = dagg
        spread(table, dagg, a_ref, 1 - row, b, (send, *more))
    total = send[:, :slab]
    for buffer in more:
        total += buffer[:, :slab]
    send[:, :slab] = total
    send[:, slab:] = jnp.concatenate(grads, 0)


def keep_kernel(slots, table, back, a_ref, dagg_ref, out_hbm, *refs):
    own, (out, sem) = refs[:-2], refs[-2:]
    row = lax.axis_index("row")
    for b in range(len(slots) // 2):
        tiles = [
            back[slots[2 * b + q], :, 2 * LANE : 3 * LANE].astype(jnp.float32) for q in range(2)
        ]
        out[:, b * LANE : (b + 1) * LANE] = jnp.concatenate(tiles, 0).astype(jnp.bfloat16)
    copy = pltpu.make_async_copy(out, out_hbm, sem)
    copy.start()
    blocks = a_ref.shape[0]
    for buffer in own:
        buffer[...] = jnp.zeros_like(buffer)
    for b in range(blocks):
        spread(table, dagg_ref[:, b * LANE : (b + 1) * LANE], a_ref, row, b, own)
    copy.wait()


def merge_kernel(scale, sent, got, *refs):
    own, (grad_features, grad_weight) = refs[:-2], refs[-2:]
    slab = grad_features.shape[1]
    total = got[:, :slab]
    for buffer in own:
        total += buffer[:, :slab]
    grad_features[...] = total.astype(jnp.bfloat16)
    grad_weight[...] = (sent[:, slab:] + got[:, slab:]) * scale


HBM, VMEM = (pl.BlockSpec(memory_space=m) for m in (pltpu.HBM, pltpu.VMEM))


def call(kernel, name, operands, outs, scratch=(), aliases=None):
    return pl.pallas_call(
        kernel,
        in_specs=[space for space, _ in operands],
        out_specs=[space for space, _, _ in outs],
        out_shape=[jax.ShapeDtypeStruct(shape, dtype) for _, shape, dtype in outs],
        scratch_shapes=list(scratch),
        input_output_aliases=aliases or {},
        compiler_params=pltpu.CompilerParams(vmem_limit_bytes=VMEM_LIMIT),
        name=name,
    )(*(array for _, array in operands))


def local(features, a_blocks, block_cols, block_counts, weight, cotangent):
    fd, slab = features.shape
    width = weight.shape[1]
    lanes = 3 * LANE + width
    ranks = lax.axis_size("col")
    slots = order(ranks)[1]
    cols, counts = block_cols.transpose(1, 2, 0), block_counts.transpose(1, 0)
    bf16, f32, i32 = jnp.bfloat16, jnp.float32, jnp.int32

    other = lax.ppermute(features, "row", SWAP)
    table, blocks, part, msg = call(
        functools.partial(first_kernel, slots),
        "first",
        [
            (HBM, pltpu.with_memory_space_constraint(x, pltpu.HBM))
            for x in (cols, counts, features, weight, cotangent, a_blocks)
        ],
        [
            (VMEM, (2, 2 * cols.shape[2], LANE), i32),
            (VMEM, a_blocks.shape, bf16),
            (VMEM, (fd, slab), f32),
            (VMEM, (ranks, fd // 2, lanes), bf16),
        ],
        [
            pltpu.VMEM((fd, slab + LANE), bf16),
            pltpu.VMEM(weight.shape, bf16),
            pltpu.VMEM(cotangent.shape, bf16),
            pltpu.VMEM(cols.shape, i32),
            pltpu.VMEM(counts.shape, i32),
            pltpu.VMEM(cols.shape, i32),
            pltpu.SMEM(cols.shape, i32),
            pltpu.SemaphoreType.DMA((5 + 2 * CHUNKS,)),
        ],
    )
    (msg,) = call(
        functools.partial(second_kernel, slots),
        "second",
        [(VMEM, x) for x in (table, other, blocks, part, msg)],
        [(VMEM, (ranks, fd // 2, lanes), bf16)],
        [pltpu.VMEM((fd, slab + LANE), bf16)],
        {4: 0},
    )
    msg = exchange(msg)
    (back,) = call(
        functools.partial(dense_kernel, slots), "dense", [(VMEM, msg)], [(VMEM, msg.shape, bf16)]
    )
    back = exchange(back)
    send, dagg = call(
        functools.partial(send_kernel, slots),
        "send",
        [(VMEM, table), (VMEM, back), (VMEM, blocks)],
        [(VMEM, (fd, slab + width), f32), (VMEM, (fd, slab), bf16)],
        [pltpu.VMEM((fd, slab + LANE), f32)] * (BUFFERS - 1),
    )
    got = lax.ppermute(send, "row", SWAP)
    output, *own = call(
        functools.partial(keep_kernel, slots),
        "keep",
        [(VMEM, x) for x in (table, back, blocks, dagg)],
        [(HBM, (fd, slab), bf16)] + [(VMEM, (fd, slab + LANE), f32)] * BUFFERS,
        [pltpu.VMEM((fd, slab), bf16), pltpu.SemaphoreType.DMA],
    )
    scale = 1.0 / (slab * lax.axis_size("row")) ** 0.5
    grad_features, grad_weight = call(
        functools.partial(merge_kernel, scale),
        "merge",
        [(VMEM, x) for x in (send, got, *own)],
        [(VMEM, (fd, slab), bf16), (VMEM, (fd, width), f32)],
    )
    return output, grad_weight, grad_features


def solution(mesh):
    placed = (
        P("col", "row"),
        P("row", None, None, None, None),
        P("row", None, None),
        P("row", None),
        P("col", None),
        P("col", "row"),
    )
    return jax.shard_map(
        local,
        mesh=mesh,
        in_specs=placed,
        out_specs=(P("col", "row"), P("col", None), P("col", "row")),
        check_vma=False,
    )
```
